32 devices in a mesh: space: 8 (over z, x), taxa: 4 (over y, core).
Axes of the slice: x: 2, y: 2, z: 4, core: 2. Of those that a mesh axis runs over, the one named last changes fastest.
Arguments:
- biomass: float32 [2048, 64, 256], P('taxa', 'space'), may hold values from 0.1 to 2
- enzymes: float32 [40, 64, 256], P(None, 'space'), may hold values from 0.1 to 1
- substrates: float32 [12, 64, 256], P(None, 'space'), may hold values from 0.5 to 5
- monomers: float32 [14, 64, 256], P(None, 'space'), may hold values from 0.1 to 2
- enz_traits: int32 [2048, 40], P('taxa'), may hold values 0 or 1
- mono_traits: int32 [2048, 14], P('taxa'), may hold values 0 or 1
- enz_target: int32 [40], replicated, may hold values from 0 to 11
- prod_rate: float32 [2048], P('taxa'), may hold values from 0.002 to 0.02
- uptake_rate: float32 [2048], P('taxa'), may hold values from 0.0005 to 0.005
- mortality: float32 [2048], P('taxa'), may hold values from 0.02 to 0.1
- disperse: float32 [2048], P('taxa'), may hold values from 0.1 to 0.5
- enz_loss: float32 [40], replicated, may hold values from 0.05 to 0.3
- vmax: float32 [40], replicated, may hold values from 0.05 to 0.5
- kmich: float32 [40], replicated, may hold values from 0.5 to 5
- khalf: float32 [14], replicated, may hold values from 0.5 to 5
- offsets: int32 [8, 2], replicated, may hold values from -2 to 2, as said below
Outputs:
- biomass_out: float32 [2048, 64, 256], P('taxa', 'space')
- enzymes_out: float32 [40, 64, 256], P(None, 'space')
- substrates_out: float32 [12, 64, 256], P(None, 'space')
- monomers_out: float32 [14, 64, 256], P(None, 'space')
The draws below stay inside these ranges and needn't reach their ends.
Inputs may be any that keep to these rules, and one draw needn't show every extreme that they name: Offsets lie in -2 to 2 in both entries and are never both zero; among the row offsets, -2 and 2 each appear twice.
All inputs are finite; a program needn't handle non-finite values. No bound on the sum of `enz_traits` or of `mono_traits` on one device may be relied on, other than what follows from the above.
Results may differ from the reference program's by a relative error of at most 0.00011.
Values sent between devices are 32-bit elements; how exact they have to be, the bound alone decides.
No kernel may reach another device: no remote copies, remote signals or barrier semaphores. Data moves between devices by JAX's collectives and lax.ppermute only.
A program may use at most 128 MiB of HBM per device.

```python
import math
import jax
import jax.numpy as jnp
from jax import lax

TAXA = 2048
ENZ = 40
SUB = 12
MONO = 14
KOFF = 8
DAYS = 2
COLS = 256
ROWS = 64


def draw_offsets(key, part):
    first, second, third = jax.random.split(jax.random.fold_in(key, 7), 3)
    base = jnp.array([-2, -1, 1, 2, -2, 0, 2, 1], jnp.int32)
    rows = base[jax.random.permutation(first, KOFF)]
    cols = jax.random.randint(second, (KOFF,), -2, 3).astype(jnp.int32)
    pick = jax.random.randint(third, (KOFF,), 0, 4).astype(jnp.int32)
    other = jnp.where(pick < 2, pick - 2, pick - 1)
    cols = jnp.where(rows == 0, other, cols)
    return jnp.stack([rows, cols], 1).astype(jnp.int32)


def plant(entries, stream_key, least, high):
    longest = entries.shape.index(max(entries.shape))
    spots = []
    for shift in (0, 1):
        where = [jax.random.randint(jax.random.fold_in(stream_key, axis), (), 0, length) for axis, length in enumerate(entries.shape)]
        where[longest] = (where[longest] + shift) % entries.shape[longest]
        spots.append(tuple(where))
    return entries.at[spots[0]].set(least).at[spots[1]].set(high)


def steps_of(own_key, extent, shards, smallest, largest):
    factor_of = 1.0
    for axis_at, shards_of in shards:
        heights = jax.random.uniform(jax.random.fold_in(jax.random.fold_in(own_key, 6), axis_at), (shards_of,), jnp.float32, smallest / len(shards), largest / len(shards))
        factor_of = factor_of * jnp.repeat(jnp.exp(heights), extent[axis_at] // shards_of).reshape((-1,) + (1,) * (len(extent) - 1 - axis_at))
    return factor_of


def setup_inputs(seed: int = 0) -> dict:
    key_of = jax.random.split(jax.random.key(seed), 17)
    biomass = jnp.clip(jnp.exp(math.log(2.0) - 2.9957323 * jax.random.uniform(key_of[0], (TAXA, ROWS, COLS), jnp.float32) ** steps_of(key_of[0], (TAXA, ROWS, COLS), ((0, 4), (1, 8)), -0.2, 0.2)), 0.1, 2.0)
    enzymes = jnp.clip(jnp.exp(math.log(1.0) - 2.3025851 * jax.random.uniform(key_of[1], (ENZ, ROWS, COLS), jnp.float32) ** steps_of(key_of[1], (ENZ, ROWS, COLS), ((1, 8),), -0.2, 0.2)), 0.1, 1.0)
    substrates = jnp.clip(jnp.exp(math.log(5.0) - 2.3025851 * jax.random.uniform(key_of[2], (SUB, ROWS, COLS), jnp.float32) ** steps_of(key_of[2], (SUB, ROWS, COLS), ((1, 8),), -0.2, 0.2)), 0.5, 5.0)
    monomers = jnp.clip(jnp.exp(math.log(2.0) - 2.9957323 * jax.random.uniform(key_of[3], (MONO, ROWS, COLS), jnp.float32) ** steps_of(key_of[3], (MONO, ROWS, COLS), ((1, 8),), -0.2, 0.2)), 0.1, 2.0)
    enz_traits = plant((jax.random.randint(key_of[4], (TAXA, ENZ), 0, 4) < 1).astype(jnp.int32), jax.random.fold_in(key_of[4], 1), 0, 1)
    mono_traits = plant((jax.random.randint(key_of[5], (TAXA, MONO), 0, 2) < 1).astype(jnp.int32), jax.random.fold_in(key_of[5], 1), 0, 1)
    enz_target = plant(jax.random.randint(key_of[6], (ENZ,), 0, SUB), jax.random.fold_in(key_of[6], 1), 0, SUB - 1).astype(jnp.int32)
    prod_rate = jnp.clip(jnp.exp(math.log(0.02) - 2.30258502 * jax.random.uniform(key_of[7], (TAXA,), jnp.float32) ** steps_of(key_of[7], (TAXA,), ((0, 4),), -0.2, 0.2)), 0.002, 0.02)
    uptake_rate = jnp.clip(jnp.exp(math.log(0.005) - 2.30258502 * jax.random.uniform(key_of[8], (TAXA,), jnp.float32) ** steps_of(key_of[8], (TAXA,), ((0, 4),), -0.2, 0.2)), 0.0005, 0.005)
    mortality = jnp.clip(0.02 + 0.08 * jax.random.uniform(key_of[9], (TAXA,), jnp.float32) ** steps_of(key_of[9], (TAXA,), ((0, 4),), -0.2, 0.2), 0.02, 0.1)
    disperse = jnp.clip(jnp.exp(math.log(0.5) - 1.609438 * jax.random.uniform(key_of[10], (TAXA,), jnp.float32) ** steps_of(key_of[10], (TAXA,), ((0, 4),), -0.2, 0.2)), 0.1, 0.5)
    enz_loss = jnp.clip(jax.random.uniform(key_of[11], (ENZ,), jnp.float32, 0.05, 0.3), 0.05, 0.3)
    vmax = jnp.clip(jnp.exp(jax.random.uniform(key_of[12], (ENZ,), jnp.float32, math.log(0.05), math.log(0.5))), 0.05, 0.5)
    kmich = jnp.clip(jnp.exp(jax.random.uniform(key_of[13], (ENZ,), jnp.float32, math.log(0.5), math.log(5.0))), 0.5, 5.0)
    khalf = jnp.clip(jnp.exp(jax.random.uniform(key_of[14], (MONO,), jnp.float32, math.log(0.5), math.log(5.0))), 0.5, 5.0)
    offsets = draw_offsets(jax.random.fold_in(key_of[16], 71), 0)
    return dict(biomass=biomass, enzymes=enzymes, substrates=substrates, monomers=monomers, enz_traits=enz_traits, mono_traits=mono_traits, enz_target=enz_target, prod_rate=prod_rate, uptake_rate=uptake_rate, mortality=mortality, disperse=disperse, enz_loss=enz_loss, vmax=vmax, kmich=kmich, khalf=khalf, offsets=offsets)


HIGH = lax.Precision.HIGHEST
YIELD = 0.6


def cell_update(sums, enz, sub, mono, enz_loss, vmax, kmich, khalf, enz_target):
    n_enz = enz.shape[0]
    made = sums[:n_enz]
    demand = sums[n_enz:]
    pool = enz * (1.0 - enz_loss)[:, None, None] + made
    pick = (enz_target[:, None] == lax.iota(jnp.int32, sub.shape[0])[None, :]).astype(jnp.float32)
    target_sub = jnp.einsum("es,srw->erw", pick, sub, precision=HIGH)
    speed = vmax[:, None, None] * pool / (kmich[:, None, None] + target_sub)
    rate = jnp.einsum("es,erw->srw", pick, speed, precision=HIGH)
    left = sub * jnp.exp(-rate)
    freed = sub - left
    extra = jnp.zeros((mono.shape[0] - sub.shape[0],) + sub.shape[1:], jnp.float32)
    mono_one = mono + jnp.concatenate([freed, extra], 0)
    share = mono_one / (khalf[:, None, None] + demand + mono_one)
    mono_two = mono_one - demand * share
    return pool, left, mono_two, share


def reference(biomass, enzymes, substrates, monomers, enz_traits, mono_traits, enz_target, prod_rate, uptake_rate, mortality, disperse, enz_loss, vmax, kmich, khalf, offsets):
    prod_w = enz_traits.astype(jnp.float32) * prod_rate[:, None]
    mono_w = mono_traits.astype(jnp.float32)
    upt_w = mono_w * uptake_rate[:, None]
    keep = 1.0 - mortality - prod_rate * jnp.sum(enz_traits.astype(jnp.float32), axis=1)
    block = min(TAXA, 128)
    blocks = TAXA // block
    bio = biomass
    for day in range(DAYS):
        flat = bio.reshape(TAXA, ROWS * COLS)
        made = jnp.dot(prod_w.T, flat, precision=HIGH, preferred_element_type=jnp.float32)
        need = jnp.dot(upt_w.T, flat, precision=HIGH, preferred_element_type=jnp.float32)
        sums = jnp.concatenate([made, need], 0).reshape(ENZ + MONO, ROWS, COLS)
        enzymes, substrates, monomers, share = cell_update(sums, enzymes, substrates, monomers, enz_loss, vmax, kmich, khalf, enz_target)

        def one_block(items):
            part_bio, part_mono, part_upt, part_keep, part_fd = items
            gain = jnp.einsum("tm,mrw->trw", part_mono, share, precision=HIGH)
            grown = part_bio * (part_keep[:, None, None] + YIELD * part_upt[:, None, None] * gain)
            moved = grown * part_fd[:, None, None]
            total = jnp.zeros_like(moved)
            for k in range(KOFF):
                total = total + jnp.roll(moved, (offsets[k, 0], offsets[k, 1]), axis=(1, 2))
            return grown - moved + total / KOFF

        bio = lax.map(one_block, (bio.reshape(blocks, block, ROWS, COLS), mono_w.reshape(blocks, block, MONO), uptake_rate.reshape(blocks, block), keep.reshape(blocks, block), disperse.reshape(blocks, block))).reshape(TAXA, ROWS, COLS)
    return bio, enzymes, substrates, monomers
```

```python
import jax
import jax.numpy as jnp
from jax import lax
from jax.experimental import pallas as pl
from jax.experimental.pallas import tpu as pltpu
from jax.sharding import PartitionSpec as P

KOFF = 8
YIELD = 0.6
HALF = 128
CHUNK = 32
SLOTS = 16
CHAN = 56
PADDED = 64
F32 = jnp.float32
BF16 = jnp.bfloat16
ANY = pl.BlockSpec(memory_space=pl.ANY)
SMEM = pl.BlockSpec(memory_space=pltpu.SMEM)
VMEM_BYTES = 40 << 20


def params():
    return pltpu.CompilerParams(vmem_limit_bytes=VMEM_BYTES)


def cost(flops, moved):
    return pl.CostEstimate(flops=flops, bytes_accessed=moved, transcendentals=0)


def pieces_outside(x, count):
    out = []
    for _ in range(count):
        part = lax.reduce_precision(x, 8, 7)
        out.append(part.astype(BF16))
        x = x - part
    return out


def pieces_inside(x, count):
    out = []
    for _ in range(count):
        part = x.astype(BF16)
        out.append(part)
        x = x - part.astype(F32)
    return out


def share_operand(share):
    high, mid, low = pieces_inside(share, 3)
    return jnp.concatenate([high, mid, low, high, mid, high], 0)


def trait_operand(matrix):
    high, mid, low = pieces_outside(matrix, 3)
    return jnp.concatenate([high, high, high, mid, mid, low], 1)


def matmul(a, b):
    return jnp.dot(a, b, preferred_element_type=F32)


def take_rows(biomass, rows):
    count, _, width = biomass.shape
    pairs = len(rows) // 2

    def kernel(source, *refs):
        outs, sem = refs[:-1], refs[-1]
        copies = [
            pltpu.make_async_copy(source.at[:, row, :], outs[i // 2].at[i % 2], sem.at[i])
            for i, row in enumerate(rows)
        ]
        for copy in copies:
            copy.start()
        for copy in copies:
            copy.wait()

    return pl.pallas_call(
        kernel,
        name="take_rows",
        out_shape=[jax.ShapeDtypeStruct((2, count, width), F32)] * pairs,
        in_specs=[ANY],
        out_specs=[ANY] * pairs,
        scratch_shapes=[pltpu.SemaphoreType.DMA((len(rows),))],
        compiler_params=params(),
        cost_estimate=cost(0, 8 * len(rows) * count * width),
    )(biomass)


def add_sums(total, row, x, weights):
    high, low = pieces_inside(x, 2)
    first = matmul(weights, high)
    second = matmul(weights[:PADDED], low)
    total[row] += first[:PADDED] + first[PADDED:] + second


def taxa_sums(row_pairs, weights, block):
    _, count, width = row_pairs[0].shape
    rows = 2 * len(row_pairs)

    def kernel(*refs):
        pairs, weight, out, total = refs[: len(row_pairs)], refs[-3], refs[-2], refs[-1]

        @pl.when(pl.program_id(0) == 0)
        def _():
            total[...] = jnp.zeros_like(total)

        for row in range(rows):
            add_sums(total, row, pairs[row // 2][row % 2], weight[...])

        @pl.when(pl.program_id(0) == pl.num_programs(0) - 1)
        def _():
            out[...] = jnp.swapaxes(total[:, :CHAN, :], 0, 1)

    return pl.pallas_call(
        kernel,
        name="taxa_sums",
        grid=(count // block,),
        out_shape=jax.ShapeDtypeStruct((CHAN, rows, width), F32),
        in_specs=[pl.BlockSpec((2, block, width), lambda i: (0, i, 0))] * len(row_pairs)
        + [pl.BlockSpec((2 * PADDED, block), lambda i: (0, i))],
        out_specs=pl.BlockSpec((CHAN, rows, width), lambda i: (0, 0, 0)),
        scratch_shapes=[pltpu.VMEM((rows, PADDED, width), F32)],
        compiler_params=params(),
        cost_estimate=cost(6 * CHAN * count * rows * width, 4 * count * rows * width),
    )(*row_pairs, weights)


def cell_update(sums, enz, sub, mono, enz_loss, vmax, kmich, khalf, enz_target):
    n_enz, rows, width = enz.shape
    n_sub, n_mono = sub.shape[0], mono.shape[0]

    def kernel(sums, enz, sub, mono, loss, vmax, kmich, khalf, target, pool, left, mono_two, out, rate, share):
        rate[...] = jnp.zeros_like(rate)

        def enzyme(e, carry):
            now = enz[e] * (1.0 - loss[e]) + sums[e]
            pool[e] = now
            at = target[e]
            rate[at] += vmax[e] * now / (kmich[e] + sub[at])
            return carry

        lax.fori_loop(0, n_enz, enzyme, 0)

        def finish(m, mono_one):
            demand = sums[n_enz + m]
            part = mono_one / (khalf[m] + demand + mono_one)
            mono_two[m] = mono_one - demand * part
            share[m] = part

        def substrate(s, carry):
            rest = sub[s] * jnp.exp(-rate[s])
            left[s] = rest
            finish(s, mono[s] + (sub[s] - rest))
            return carry

        lax.fori_loop(0, n_sub, substrate, 0)
        for m in range(n_sub, n_mono):
            finish(m, mono[m])
        share[n_mono] = jnp.ones((rows, width), F32)
        for m in range(n_mono + 1, SLOTS):
            share[m] = jnp.zeros((rows, width), F32)
        out[...] = jnp.swapaxes(share[...], 0, 1)

    whole = pl.BlockSpec(memory_space=pltpu.VMEM)
    return pl.pallas_call(
        kernel,
        name="cell_update",
        out_shape=[
            jax.ShapeDtypeStruct(enz.shape, F32),
            jax.ShapeDtypeStruct(sub.shape, F32),
            jax.ShapeDtypeStruct(mono.shape, F32),
            jax.ShapeDtypeStruct((rows, SLOTS, width), F32),
        ],
        in_specs=[whole] * 4 + [SMEM] * 5,
        out_specs=[whole] * 4,
        scratch_shapes=[pltpu.VMEM(sub.shape, F32), pltpu.VMEM((SLOTS, rows, width), F32)],
        compiler_params=params(),
        cost_estimate=cost(20 * n_enz * rows * width, 8 * 2 * n_enz * rows * width),
    )(sums, enz, sub, mono, enz_loss, vmax, kmich, khalf, enz_target)


def lanes():
    return lax.broadcasted_iota(jnp.int32, (CHUNK, HALF), 1)


def shifted(ref, row, taxa, by, lane):
    first = pltpu.roll(ref[row, taxa, :HALF], jnp.where(by < 0, by + HALF, by), 1)
    second = pltpu.roll(ref[row, taxa, HALF:], jnp.where(by < 0, by + HALF, by), 1)
    crossed = (lane < by) | (lane >= HALF + by)
    return jnp.where(crossed, second, first), jnp.where(crossed, first, second)


def full_stencil(moved, result, offsets, rows, first_row, block):
    lane = lanes()
    steps = block // CHUNK

    def body(i, carry):
        row = i // steps
        taxa = pl.ds(pl.multiple_of((i % steps) * CHUNK, CHUNK), CHUNK)
        left = result[row, taxa, :HALF]
        right = result[row, taxa, HALF:]
        for k in range(KOFF):
            a, b = shifted(moved, row + first_row - offsets[k, 0], taxa, offsets[k, 1], lane)
            left += a
            right += b
        result[row, taxa, :HALF] = left
        result[row, taxa, HALF:] = right
        return carry

    lax.fori_loop(0, rows * steps, body, 0)


def day_one(row_pairs, low, high, share, share_low, share_high, to_moved, to_kept, weights, offsets, block):
    _, count, width = low.shape
    rows = 2 * len(row_pairs)
    ext = rows + 4

    def kernel(*refs):
        pairs = refs[: len(row_pairs) + 2]
        own, before, after, moved_w, kept_w, weight, offs, out, sums, moved, total = refs[len(row_pairs) + 2 :]

        @pl.when(pl.program_id(0) == 0)
        def _():
            total[...] = jnp.zeros_like(total)
            for row in (0, 1, ext + 2, ext + 3):
                moved[row] = jnp.zeros((block, width), F32)

        for row in range(ext):
            x = pairs[row // 2][row % 2]
            if row < 2:
                part = before[2 + row]
            elif row < 2 + rows:
                part = own[row - 2]
            else:
                part = after[row - 2 - rows]
            part = share_operand(part)
            moved[row + 2] = x * matmul(moved_w[...], part)
            out[row] = x * matmul(kept_w[...], part)
        full_stencil(moved, out, offs, ext, 2, block)

        def add(row, carry):
            add_sums(total, row, out[row + 2], weight[...])
            return carry

        lax.fori_loop(0, rows, add, 0)

        @pl.when(pl.program_id(0) == pl.num_programs(0) - 1)
        def _():
            sums[...] = jnp.swapaxes(total[:, :CHAN, :], 0, 1)

    def whole(shape):
        return pl.BlockSpec(shape, lambda i: (0,) * len(shape))

    operand = to_moved.shape[1]
    return pl.pallas_call(
        kernel,
        name="day_one",
        grid=(count // block,),
        out_shape=[
            jax.ShapeDtypeStruct((ext, count, width), F32),
            jax.ShapeDtypeStruct((CHAN, rows, width), F32),
        ],
        in_specs=[pl.BlockSpec((2, block, width), lambda i: (0, i, 0))] * (len(row_pairs) + 2)
        + [
            whole(share.shape),
            whole(share_low.shape),
            whole(share_high.shape),
            pl.BlockSpec((block, operand), lambda i: (i, 0)),
            pl.BlockSpec((block, operand), lambda i: (i, 0)),
            pl.BlockSpec((2 * PADDED, block), lambda i: (0, i)),
            SMEM,
        ],
        out_specs=[
            pl.BlockSpec((ext, block, width), lambda i: (0, i, 0)),
            whole((CHAN, rows, width)),
        ],
        scratch_shapes=[
            pltpu.VMEM((ext + 4, block, width), F32),
            pltpu.VMEM((rows, PADDED, width), F32),
        ],
        compiler_params=params(),
        cost_estimate=cost(60 * count * ext * width, 8 * count * ext * width),
    )(low, *row_pairs, high, share, share_low, share_high, to_moved, to_kept, weights, offsets)


def day_two(grown, share, to_moved, to_kept, offsets, block):
    ext, count, width = grown.shape
    rows = ext - 4
    steps = count // block

    def kernel(x, own, moved_w, kept_w, offs, out, edge, moved, result, sem):
        step = pl.program_id(0)
        slot = lax.rem(step, 2)

        def copies(at, where):
            found = []
            taxa = pl.ds(pl.multiple_of(at * block, block), block)
            for row in range(rows):
                if 2 <= row < rows - 2:
                    target = out.at[taxa, row, :]
                else:
                    target = edge.at[row if row < 2 else row - rows + 4, taxa, :]
                found.append(pltpu.make_async_copy(result.at[where, row], target, sem.at[where, row]))
            return found

        @pl.when(step == 0)
        def _():
            for row in (0, 1, ext - 2, ext - 1):
                moved[row] = jnp.zeros((block, width), F32)

        @pl.when(step >= 2)
        def _():
            for copy in copies(step - 2, slot):
                copy.wait()

        for row in range(rows):
            part = share_operand(own[row])
            value = x[row + 2]
            moved[row + 2] = value * matmul(moved_w[...], part)
            result[slot, row] = value * matmul(kept_w[...], part)
        full_stencil(moved, result.at[slot], offs, rows, 2, block)
        for copy in copies(step, slot):
            copy.start()

        @pl.when(step == steps - 1)
        def _():
            if steps > 1:
                for copy in copies(step - 1, 1 - slot):
                    copy.wait()
            for copy in copies(step, slot):
                copy.wait()

    operand = to_moved.shape[1]
    return pl.pallas_call(
        kernel,
        name="day_two",
        grid=(steps,),
        out_shape=[
            jax.ShapeDtypeStruct((count, rows, width), F32),
            jax.ShapeDtypeStruct((4, count, width), F32),
        ],
        in_specs=[
            pl.BlockSpec((ext, block, width), lambda i: (0, i, 0)),
            pl.BlockSpec(share.shape, lambda i: (0, 0, 0)),
            pl.BlockSpec((block, operand), lambda i: (i, 0)),
            pl.BlockSpec((block, operand), lambda i: (i, 0)),
            SMEM,
        ],
        out_specs=[ANY, ANY],
        scratch_shapes=[
            pltpu.VMEM((ext, block, width), F32),
            pltpu.VMEM((2, rows, block, width), F32),
            pltpu.SemaphoreType.DMA((2, rows)),
        ],
        compiler_params=params(),
        cost_estimate=cost(60 * count * rows * width, 8 * count * rows * width),
    )(grown, share, to_moved, to_kept, offsets)


def edges(outer_low, outer_high, grown, edge, biomass_out, day_one_share, day_two_share, to_moved, offsets, block):
    _, count, width = outer_low.shape
    rows = biomass_out.shape[1]
    last = grown.shape[0] // 2 - 1
    steps = count // block
    chunks = block // CHUNK

    def kernel(low, high, near_low, near_high, own, s1, s2, moved_w, offs, unused, out, far, near, result, lists, counts, sem):
        step = pl.program_id(0)
        slot = lax.rem(step, 2)
        lane = lanes()

        @pl.when(step == 0)
        def _():
            for i in range(4):
                counts[i] = 0
            for k in range(KOFF):
                for i, value in enumerate((2, 1, -1, -2)):

                    @pl.when(offs[k, 0] == value)
                    def _():
                        lists[i, counts[i]] = offs[k, 1]
                        counts[i] = counts[i] + 1

        def copies(at, where):
            taxa = pl.ds(pl.multiple_of(at * block, block), block)
            return [
                pltpu.make_async_copy(
                    result.at[where, i],
                    out.at[taxa, i if i < 2 else rows - 4 + i, :],
                    sem.at[where, i],
                )
                for i in range(4)
            ]

        @pl.when(step >= 2)
        def _():
            for copy in copies(step - 2, slot):
                copy.wait()

        for i in range(4):
            x = low[i] if i < 2 else high[i - 2]
            far[i] = x * matmul(moved_w[...], share_operand(s1[i]))

        def gather(ref, row, which, taxa, pair):
            def body(k, carry):
                a, b = shifted(ref, row, taxa, lists[which, k], lane)
                return carry[0] + a, carry[1] + b

            return lax.fori_loop(0, counts[which], body, pair)

        def sides(source, base, target, terms):
            def body(i, carry):
                taxa = pl.ds(pl.multiple_of(i * CHUNK, CHUNK), CHUNK)
                for row, parts in enumerate(terms):
                    pair = base(row, taxa)
                    for origin, which in parts:
                        pair = gather(source, origin, which, taxa, pair)
                    target(row, taxa, pair)
                return carry

            lax.fori_loop(0, chunks, body, 0)

        def near_base(row, taxa):
            ref = near_low if row < 2 else near_high
            return ref[row % 2, taxa, :HALF], ref[row % 2, taxa, HALF:]

        def near_store(row, taxa, pair):
            near[row, taxa, :HALF] = pair[0]
            near[row, taxa, HALF:] = pair[1]

        def own_base(row, taxa):
            return own[row, taxa, :HALF], own[row, taxa, HALF:]

        def own_store(row, taxa, pair):
            result[slot, row, taxa, :HALF] = pair[0]
            result[slot, row, taxa, HALF:] = pair[1]

        two, one, minus_one, minus_two = range(4)
        terms = (
            ((0, two), (1, one)),
            ((1, two),),
            ((2, minus_two),),
            ((3, minus_two), (2, minus_one)),
        )
        sides(far, near_base, near_store, terms)
        for i in range(4):
            near[i] = near[i] * matmul(moved_w[...], share_operand(s2[i]))
        sides(near, own_base, own_store, terms)
        for copy in copies(step, slot):
            copy.start()

        @pl.when(step == steps - 1)
        def _():
            if steps > 1:
                for copy in copies(step - 1, 1 - slot):
                    copy.wait()
            for copy in copies(step, slot):
                copy.wait()

    operand = to_moved.shape[1]
    pair = (2, block, width)
    return pl.pallas_call(
        kernel,
        name="edges",
        grid=(steps,),
        out_shape=jax.ShapeDtypeStruct(biomass_out.shape, F32),
        in_specs=[
            pl.BlockSpec(pair, lambda i: (0, i, 0)),
            pl.BlockSpec(pair, lambda i: (0, i, 0)),
            pl.BlockSpec(pair, lambda i: (0, i, 0)),
            pl.BlockSpec(pair, lambda i: (last, i, 0)),
            pl.BlockSpec((4, block, width), lambda i: (0, i, 0)),
            pl.BlockSpec(day_one_share.shape, lambda i: (0, 0, 0)),
            pl.BlockSpec(day_two_share.shape, lambda i: (0, 0, 0)),
            pl.BlockSpec((block, operand), lambda i: (i, 0)),
            SMEM,
            ANY,
        ],
        out_specs=ANY,
        scratch_shapes=[
            pltpu.VMEM((4, block, width), F32),
            pltpu.VMEM((4, block, width), F32),
            pltpu.VMEM((2, 4, block, width), F32),
            pltpu.SMEM((4, KOFF), jnp.int32),
            pltpu.SMEM((4,), jnp.int32),
            pltpu.SemaphoreType.DMA((2, 4)),
        ],
        input_output_aliases={9: 0},
        compiler_params=params(),
        cost_estimate=cost(60 * count * 4 * width, 8 * count * 8 * width),
    )(outer_low, outer_high, grown, grown, edge, day_one_share, day_two_share, to_moved, offsets, biomass_out)


def over_taxa(value):
    count = lax.axis_size("taxa")
    step = 1
    while step < count:
        value = value + lax.ppermute(value, "taxa", [(i, i ^ step) for i in range(count)])
        step *= 2
    return value


def body(
    biomass,
    enzymes,
    substrates,
    monomers,
    enz_traits,
    mono_traits,
    enz_target,
    prod_rate,
    uptake_rate,
    mortality,
    disperse,
    enz_loss,
    vmax,
    kmich,
    khalf,
    offsets,
):
    ring = lax.axis_size("space")
    forward = [(i, (i + 1) % ring) for i in range(ring)]
    backward = [(target, source) for source, target in forward]

    def down(x):
        return lax.ppermute(x, "space", forward)

    def up(x):
        return lax.ppermute(x, "space", backward)

    count, rows, width = biomass.shape
    block = min(count, 256)

    first, last = take_rows(biomass, (0, 1, rows - 2, rows - 1))
    inner_low, inner_high = down(last), up(first)
    middle = take_rows(biomass, tuple(range(2, rows - 2)))
    row_pairs = [first, *middle, last]

    enz_f = enz_traits.astype(F32)
    mono_f = mono_traits.astype(F32)
    weight = jnp.concatenate(
        [
            enz_f * prod_rate[:, None],
            mono_f * uptake_rate[:, None],
            jnp.zeros((count, PADDED - enz_f.shape[1] - mono_f.shape[1]), F32),
        ],
        1,
    ).T
    weights = jnp.concatenate(pieces_outside(weight, 2), 0)
    keep = 1.0 - mortality - prod_rate * jnp.sum(enz_f, axis=1)
    gain = jnp.concatenate(
        [
            (YIELD * uptake_rate)[:, None] * mono_f,
            keep[:, None],
            jnp.zeros((count, SLOTS - 1 - mono_f.shape[1]), F32),
        ],
        1,
    )
    to_moved = trait_operand(gain * (disperse / KOFF)[:, None])
    to_kept = trait_operand(gain * (1.0 - disperse)[:, None])
    cells = (enz_loss, vmax, kmich, khalf, enz_target)

    sums = over_taxa(taxa_sums(row_pairs, weights, block))
    enzymes, substrates, monomers, share_one = cell_update(sums, enzymes, substrates, monomers, *cells)
    share_low, share_high = down(share_one[rows - 4 :]), up(share_one[:4])

    inner_low, inner_high, outer_first, outer_last = lax.optimization_barrier(
        (inner_low, inner_high, middle[0], middle[-1])
    )
    outer_low, outer_high = down(outer_last), up(outer_first)
    grown, sums = day_one(
        row_pairs, inner_low, inner_high, share_one, share_low, share_high, to_moved, to_kept, weights, offsets, block
    )
    sums = over_taxa(sums)
    enzymes, substrates, monomers, share_two = cell_update(sums, enzymes, substrates, monomers, *cells)
    near_low, near_high = down(share_two[rows - 2 :]), up(share_two[:2])
    biomass_out, edge = day_two(grown, share_two, to_moved, to_kept, offsets, block)
    biomass_out = edges(
        outer_low,
        outer_high,
        grown,
        edge,
        biomass_out,
        jnp.concatenate([share_low[:2], share_high[2:]], 0),
        jnp.concatenate([near_low, near_high], 0),
        to_moved,
        offsets,
        min(count, 128),
    )
    return (biomass_out, enzymes, substrates, monomers)


def solution(mesh):
    placed = (
        P("taxa", "space", None),
        P(None, "space", None),
        P(None, "space", None),
        P(None, "space", None),
        P("taxa", None),
        P("taxa", None),
        P(),
        P("taxa"),
        P("taxa"),
        P("taxa"),
        P("taxa"),
        P(),
        P(),
        P(),
        P(),
        P(),
    )
    return jax.shard_map(
        body,
        mesh=mesh,
        in_specs=placed,
        out_specs=(
            P("taxa", "space", None),
            P(None, "space", None),
            P(None, "space", None),
            P(None, "space", None),
        ),
        check_vma=False,
    )
```

```python
import jax
import jax.numpy as jnp
from jax import lax
from jax.experimental import pallas as pl
from jax.experimental.pallas import tpu as pltpu
from jax.sharding import PartitionSpec as P

KOFF = 8
YIELD = 0.6
HALF = 128
SLOTS = 16
CHAN = 56
PADDED = 64
F32 = jnp.float32
BF16 = jnp.bfloat16
ANY = pl.BlockSpec(memory_space=pl.ANY)
SMEM = pl.BlockSpec(memory_space=pltpu.SMEM)
VMEM_BYTES = 40 << 20


def params():
    return pltpu.CompilerParams(vmem_limit_bytes=VMEM_BYTES)


def cost(flops, moved):
    return pl.CostEstimate(flops=flops, bytes_accessed=moved, transcendentals=0)


def pieces_outside(x, count):
    out = []
    for _ in range(count):
        part = lax.reduce_precision(x, 8, 7)
        out.append(part.astype(BF16))
        x = x - part
    return out


def pieces_inside(x, count):
    out = []
    for _ in range(count):
        part = x.astype(BF16)
        out.append(part)
        x = x - part.astype(F32)
    return out


def share_operand(share):
    high, mid, low = pieces_inside(share, 3)
    return jnp.concatenate([high, mid, low, high, mid, high], 0)


def trait_operand(matrix):
    high, mid, low = pieces_outside(matrix, 3)
    return jnp.concatenate([high, high, high, mid, mid, low], 1)


def matmul(a, b):
    return jnp.dot(a, b, preferred_element_type=F32)


def take_rows(biomass, rows):
    count, _, width = biomass.shape
    pairs = len(rows) // 2

    def kernel(source, *refs):
        outs, sem = refs[:-1], refs[-1]
        copies = [
            pltpu.make_async_copy(source.at[:, row, :], outs[i // 2].at[i % 2], sem.at[i])
            for i, row in enumerate(rows)
        ]
        for copy in copies:
            copy.start()
        for copy in copies:
            copy.wait()

    return pl.pallas_call(
        kernel,
        name="take_rows",
        out_shape=[jax.ShapeDtypeStruct((2, count, width), F32)] * pairs,
        in_specs=[ANY],
        out_specs=[ANY] * pairs,
        scratch_shapes=[pltpu.SemaphoreType.DMA((len(rows),))],
        compiler_params=params(),
        cost_estimate=cost(0, 8 * len(rows) * count * width),
    )(biomass)


def add_sums(total, row, x, weights):
    high, low = pieces_inside(x, 2)
    first = matmul(weights, high)
    second = matmul(weights[:PADDED], low)
    total[row] += first[:PADDED] + first[PADDED:] + second


def finish_sums(total, odd, mine, other):
    low = jnp.swapaxes(total[:, : CHAN // 2, :], 0, 1)
    high = jnp.swapaxes(total[:, CHAN // 2 : CHAN, :], 0, 1)

    @pl.when(odd[0] == 0)
    def _():
        mine[...] = low
        other[...] = high

    @pl.when(odd[0] != 0)
    def _():
        mine[...] = high
        other[...] = low


def taxa_sums(row_pairs, weights, odd, block):
    _, count, width = row_pairs[0].shape
    rows = 2 * len(row_pairs)

    def kernel(*refs):
        pairs = refs[: len(row_pairs)]
        weight, side, mine, other, total = refs[len(row_pairs) :]

        @pl.when(pl.program_id(0) == 0)
        def _():
            total[...] = jnp.zeros_like(total)

        for row in range(rows):
            add_sums(total, row, pairs[row // 2][row % 2], weight[...])

        @pl.when(pl.program_id(0) == pl.num_programs(0) - 1)
        def _():
            finish_sums(total, side, mine, other)

    half = (CHAN // 2, rows, width)
    return pl.pallas_call(
        kernel,
        name="taxa_sums",
        grid=(count // block,),
        out_shape=[jax.ShapeDtypeStruct(half, F32)] * 2,
        in_specs=[pl.BlockSpec((2, block, width), lambda i: (0, i, 0))] * len(row_pairs)
        + [pl.BlockSpec((2 * PADDED, block), lambda i: (0, i)), SMEM],
        out_specs=[whole(half)] * 2,
        scratch_shapes=[pltpu.VMEM((rows, PADDED, width), F32)],
        compiler_params=params(),
        cost_estimate=cost(1000, 1000),
    )(*row_pairs, weights, odd)


def cell_update(mine, rest, odd, enz, sub, mono, enz_loss, vmax, kmich, khalf, enz_target):
    n_enz, rows, width = enz.shape
    n_sub, n_mono = sub.shape[0], mono.shape[0]

    def kernel(*refs):
        mine, rest, enz, sub, mono, side, loss, vmax, kmich, khalf, target = refs[:11]
        pool, left, mono_two, out, sums, speed, rate, share = refs[11:]
        half = mine.shape[0]

        @pl.when(side[0] == 0)
        def _():
            sums[:half] = mine[...]
            sums[half:] = rest[...]

        @pl.when(side[0] != 0)
        def _():
            sums[:half] = rest[...]
            sums[half:] = mine[...]

        rate[...] = jnp.zeros_like(rate)
        for e in range(n_enz):
            now = enz[e] * (1.0 - loss[e]) + sums[e]
            pool[e] = now
            speed[e] = vmax[e] * now / (kmich[e] + sub[target[e]])
        for e in range(n_enz):
            rate[target[e]] += speed[e]

        def finish(m, mono_one):
            demand = sums[n_enz + m]
            part = mono_one / (khalf[m] + demand + mono_one)
            mono_two[m] = mono_one - demand * part
            share[m] = part

        for s in range(n_sub):
            kept = sub[s] * jnp.exp(-rate[s])
            left[s] = kept
            finish(s, mono[s] + (sub[s] - kept))
        for m in range(n_sub, n_mono):
            finish(m, mono[m])
        share[n_mono] = jnp.ones((rows, width), F32)
        for m in range(n_mono + 1, SLOTS):
            share[m] = jnp.zeros((rows, width), F32)
        out[...] = jnp.swapaxes(share[...], 0, 1)

    vmem = pl.BlockSpec(memory_space=pltpu.VMEM)
    return pl.pallas_call(
        kernel,
        name="cell_update",
        out_shape=[
            jax.ShapeDtypeStruct(enz.shape, F32),
            jax.ShapeDtypeStruct(sub.shape, F32),
            jax.ShapeDtypeStruct(mono.shape, F32),
            jax.ShapeDtypeStruct((rows, SLOTS, width), F32),
        ],
        in_specs=[vmem] * 5 + [SMEM] * 6,
        out_specs=[vmem] * 4,
        scratch_shapes=[
            pltpu.VMEM((CHAN, rows, width), F32),
            pltpu.VMEM(enz.shape, F32),
            pltpu.VMEM(sub.shape, F32),
            pltpu.VMEM((SLOTS, rows, width), F32),
        ],
        compiler_params=params(),
        cost_estimate=cost(1000, 1000),
    )(mine, rest, enz, sub, mono, odd, enz_loss, vmax, kmich, khalf, enz_target)


def circulants(offsets, width):
    row_offset = 2 - lax.iota(jnp.int32, 5)
    col_offset = lax.iota(jnp.int32, 5) - 2
    row_hit = (offsets[:, 0, None] == row_offset[None, :]).astype(F32)
    col_hit = (offsets[:, 1, None] == col_offset[None, :]).astype(F32)
    number = jnp.sum(row_hit[:, :, None] * col_hit[:, None, :], axis=0)
    still = (row_offset[:, None] == 0) & (col_offset[None, :] == 0)
    number = number - KOFF * still.astype(F32)
    source = lax.broadcasted_iota(jnp.int32, (width, width), 0)
    target = lax.broadcasted_iota(jnp.int32, (width, width), 1)
    apart = lax.rem(target - source + width + 2, width)
    total = jnp.zeros((5, width, width), F32)
    for i in range(5):
        total = total + number[:, i, None, None] * (apart == i).astype(F32)
    total = jnp.broadcast_to(total.astype(BF16)[:, None], (5, 2, width, width))
    return total.reshape(10 * width, width)


def store_pieces(pieces, index, value):
    width = value.shape[1]
    at = 2 * width * index
    high, low = pieces_inside(value, 2)
    pieces[:, at : at + width] = high
    pieces[:, at + width : at + 2 * width] = low


def stencil(pieces, circulant, first, count, offset):
    span = circulant.shape[1] * 2
    return matmul(
        pieces[:, span * first : span * (first + count)],
        circulant[span * offset : span * (offset + count), :],
    )


def window(target, rows):
    first = max(target - 2, 0)
    return first, min(target + 2, rows - 1) - first + 1, first - target + 2


def spread(value, fraction, change):
    return value + jnp.concatenate([fraction, fraction], 1) * change


def whole(shape):
    return pl.BlockSpec(shape, lambda i: (0,) * len(shape))


def pair_spec(block, width, at=0):
    return pl.BlockSpec((2, block, width), lambda i: (at, i, 0))


def taxa_spec(block, width):
    return pl.BlockSpec((block, width), lambda i: (i, 0))


def day_one_inside(row_pairs, share, gain, fraction, circulant, weights, block):
    _, count, width = row_pairs[0].shape
    rows = 2 * len(row_pairs)
    inner = rows - 4

    def kernel(*refs):
        pairs = refs[: len(row_pairs)]
        own, gain_w, frac, circ, weight, out, total, pieces = refs[len(row_pairs) :]

        @pl.when(pl.program_id(0) == 0)
        def _():
            total[...] = jnp.zeros_like(total)

        for row in range(rows):
            value = pairs[row // 2][row % 2] * matmul(gain_w[...], share_operand(own[row]))
            out[row] = value
            store_pieces(pieces, row, value)
        for row in range(rows):
            value = spread(out[row], frac[...], stencil(pieces, circ, *window(row, rows)))
            out[row] = value
            if 2 <= row < rows - 2:
                add_sums(total, row - 2, value, weight[...])

    return pl.pallas_call(
        kernel,
        name="day_one_inside",
        grid=(count // block,),
        out_shape=[
            jax.ShapeDtypeStruct((rows, count, width), F32),
            jax.ShapeDtypeStruct((inner, PADDED, width), F32),
        ],
        in_specs=[pair_spec(block, width)] * len(row_pairs)
        + [
            whole(share.shape),
            taxa_spec(block, gain.shape[1]),
            taxa_spec(block, HALF),
            whole(circulant.shape),
            pl.BlockSpec((2 * PADDED, block), lambda i: (0, i)),
        ],
        out_specs=[
            pl.BlockSpec((rows, block, width), lambda i: (0, i, 0)),
            whole((inner, PADDED, width)),
        ],
        scratch_shapes=[pltpu.VMEM((block, rows * 2 * width), BF16)],
        compiler_params=params(),
        cost_estimate=cost(1000, 1000),
    )(*row_pairs, share, gain, fraction, circulant, weights)


TERMS = ((0, 2, 0), (1, 1, 0), (2, 1, 4), (2, 2, 3))


def day_one_rim(low, high, inside, sums, share_low, share_high, gain, fraction, circulant, weights, odd, block):
    _, count, width = low.shape
    rows = inside.shape[0]

    def kernel(
        low, high, first, last, part, before, after, gain_w, frac, circ, weight, side, out, mine, other, far, total
    ):
        @pl.when(pl.program_id(0) == 0)
        def _():
            total[2 : rows - 2] = part[...]
            for row in (0, 1, rows - 2, rows - 1):
                total[row] = jnp.zeros((PADDED, width), F32)

        for i in range(4):
            x = low[i] if i < 2 else high[i - 2]
            s = before[2 + i] if i < 2 else after[i - 2]
            store_pieces(far, i, x * matmul(gain_w[...], share_operand(s)))
        for i in range(4):
            x = first[i] if i < 2 else last[i - 2]
            value = spread(x, frac[...], stencil(far, circ, *TERMS[i]))
            out[i] = value
            add_sums(total, i if i < 2 else rows - 4 + i, value, weight[...])

        @pl.when(pl.program_id(0) == pl.num_programs(0) - 1)
        def _():
            finish_sums(total, side, mine, other)

    half = (CHAN // 2, rows, width)
    return pl.pallas_call(
        kernel,
        name="day_one_rim",
        grid=(count // block,),
        out_shape=[jax.ShapeDtypeStruct((4, count, width), F32)] + [jax.ShapeDtypeStruct(half, F32)] * 2,
        in_specs=[
            pair_spec(block, width),
            pair_spec(block, width),
            pair_spec(block, width),
            pair_spec(block, width, rows // 2 - 1),
            whole(sums.shape),
            whole(share_low.shape),
            whole(share_high.shape),
            taxa_spec(block, gain.shape[1]),
            taxa_spec(block, HALF),
            whole(circulant.shape),
            pl.BlockSpec((2 * PADDED, block), lambda i: (0, i)),
            SMEM,
        ],
        out_specs=[pl.BlockSpec((4, block, width), lambda i: (0, i, 0))] + [whole(half)] * 2,
        scratch_shapes=[
            pltpu.VMEM((block, 8 * width), BF16),
            pltpu.VMEM((rows, PADDED, width), F32),
        ],
        compiler_params=params(),
        cost_estimate=cost(1000, 1000),
    )(low, high, inside, inside, sums, share_low, share_high, gain, fraction, circulant, weights, odd)


def day_one_beyond(row_pairs, low, high, share, share_low, share_high, gain, fraction, circulant, block):
    _, count, width = low.shape
    rows = 2 * len(row_pairs)

    def kernel(low, high, first, last, own, before, after, gain_w, frac, circ, out, pieces):
        for side in range(2):
            for i in range(4):
                if side == 0:
                    x = low[i] if i < 2 else first[i - 2]
                    s = before[2 + i] if i < 2 else own[i - 2]
                else:
                    x = last[i] if i < 2 else high[i - 2]
                    s = own[rows - 2 + i] if i < 2 else after[i - 2]
                value = x * matmul(gain_w[...], share_operand(s))
                store_pieces(pieces, i, value)
                if (i < 2) == (side == 0):
                    out[i] = value
            for i in (0, 1) if side == 0 else (2, 3):
                out[i] = spread(out[i], frac[...], stencil(pieces, circ, *window(i, 4)))

    return pl.pallas_call(
        kernel,
        name="day_one_beyond",
        grid=(count // block,),
        out_shape=jax.ShapeDtypeStruct((4, count, width), F32),
        in_specs=[pair_spec(block, width)] * 4
        + [
            whole(share.shape),
            whole(share_low.shape),
            whole(share_high.shape),
            taxa_spec(block, gain.shape[1]),
            taxa_spec(block, HALF),
            whole(circulant.shape),
        ],
        out_specs=pl.BlockSpec((4, block, width), lambda i: (0, i, 0)),
        scratch_shapes=[pltpu.VMEM((block, 8 * width), BF16)],
        compiler_params=params(),
        cost_estimate=cost(1000, 1000),
    )(low, high, row_pairs[0], row_pairs[-1], share, share_low, share_high, gain, fraction, circulant)


def day_two(inside, rim, share, gain, fraction, circulant, block):
    rows, count, width = inside.shape
    steps = count // block
    middle = rows // 2 - 2

    def kernel(*refs):
        inner = refs[:middle]
        outer, own, gain_w, frac, circ, out, edge, pieces, result, sem = refs[middle:]
        step = pl.program_id(0)
        slot = lax.rem(step, 2)

        def copies(at, where):
            found = []
            taxa = pl.ds(pl.multiple_of(at * block, block), block)
            for row in range(rows):
                if 2 <= row < rows - 2:
                    target = out.at[taxa, row, :]
                else:
                    target = edge.at[row if row < 2 else row - rows + 4, taxa, :]
                found.append(pltpu.make_async_copy(result.at[where, row], target, sem.at[where, row]))
            return found

        @pl.when(step >= 2)
        def _():
            for copy in copies(step - 2, slot):
                copy.wait()

        for row in range(rows):
            if 2 <= row < rows - 2:
                x = inner[row // 2 - 1][row % 2]
            else:
                x = outer[row if row < 2 else row - rows + 4]
            value = x * matmul(gain_w[...], share_operand(own[row]))
            result[slot, row] = value
            store_pieces(pieces, row, value)
        for row in range(rows):
            result[slot, row] = spread(result[slot, row], frac[...], stencil(pieces, circ, *window(row, rows)))
        for copy in copies(step, slot):
            copy.start()

        @pl.when(step == steps - 1)
        def _():
            if steps > 1:
                for copy in copies(step - 1, 1 - slot):
                    copy.wait()
            for copy in copies(step, slot):
                copy.wait()

    return pl.pallas_call(
        kernel,
        name="day_two",
        grid=(steps,),
        out_shape=[
            jax.ShapeDtypeStruct((count, rows, width), F32),
            jax.ShapeDtypeStruct((4, count, width), F32),
        ],
        in_specs=[
            *[pair_spec(block, width, 1 + i) for i in range(middle)],
            pl.BlockSpec((4, block, width), lambda i: (0, i, 0)),
            whole(share.shape),
            taxa_spec(block, gain.shape[1]),
            taxa_spec(block, HALF),
            whole(circulant.shape),
        ],
        out_specs=[ANY, ANY],
        scratch_shapes=[
            pltpu.VMEM((block, rows * 2 * width), BF16),
            pltpu.VMEM((2, rows, block, width), F32),
            pltpu.SemaphoreType.DMA((2, rows)),
        ],
        compiler_params=params(),
        cost_estimate=cost(1000, 1000),
    )(*[inside] * middle, rim, share, gain, fraction, circulant)


def edges(outer_low, outer_high, beyond, edge, biomass_out, share_one, share_two, gain, fraction, circulant, block):
    _, count, width = outer_low.shape
    rows = biomass_out.shape[1]
    steps = count // block

    def kernel(low, high, near_low, near_high, own, s1, s2, gain_w, frac, circ, unused, out, far, near, result, sem):
        step = pl.program_id(0)
        slot = lax.rem(step, 2)

        def copies(at, where):
            taxa = pl.ds(pl.multiple_of(at * block, block), block)
            return [
                pltpu.make_async_copy(
                    result.at[where, i],
                    out.at[taxa, i if i < 2 else rows - 4 + i, :],
                    sem.at[where, i],
                )
                for i in range(4)
            ]

        @pl.when(step >= 2)
        def _():
            for copy in copies(step - 2, slot):
                copy.wait()

        for i in range(4):
            x = low[i] if i < 2 else high[i - 2]
            store_pieces(far, i, x * matmul(gain_w[...], share_operand(s1[i])))
        for i in range(4):
            x = near_low[i] if i < 2 else near_high[i - 2]
            value = spread(x, frac[...], stencil(far, circ, *TERMS[i]))
            store_pieces(near, i, value * matmul(gain_w[...], share_operand(s2[i])))
        for i in range(4):
            result[slot, i] = spread(own[i], frac[...], stencil(near, circ, *TERMS[i]))
        for copy in copies(step, slot):
            copy.start()

        @pl.when(step == steps - 1)
        def _():
            if steps > 1:
                for copy in copies(step - 1, 1 - slot):
                    copy.wait()
            for copy in copies(step, slot):
                copy.wait()

    return pl.pallas_call(
        kernel,
        name="edges",
        grid=(steps,),
        out_shape=jax.ShapeDtypeStruct(biomass_out.shape, F32),
        in_specs=[
            *[pair_spec(block, width)] * 3,
            pair_spec(block, width, 1),
            pl.BlockSpec((4, block, width), lambda i: (0, i, 0)),
            whole(share_one.shape),
            whole(share_two.shape),
            pl.BlockSpec((block, gain.shape[1]), lambda i: (i, 0)),
            pl.BlockSpec((block, HALF), lambda i: (i, 0)),
            whole(circulant.shape),
            ANY,
        ],
        out_specs=ANY,
        scratch_shapes=[
            pltpu.VMEM((block, 8 * width), BF16),
            pltpu.VMEM((block, 8 * width), BF16),
            pltpu.VMEM((2, 4, block, width), F32),
            pltpu.SemaphoreType.DMA((2, 4)),
        ],
        input_output_aliases={10: 0},
        compiler_params=params(),
        cost_estimate=cost(1000, 1000),
    )(outer_low, outer_high, beyond, beyond, edge, share_one, share_two, gain, fraction, circulant, biomass_out)


def over_taxa(mine, other):
    count = lax.axis_size("taxa")

    def exchange(x, step):
        return lax.ppermute(x, "taxa", [(i, i ^ step) for i in range(count)])

    mine = mine + exchange(other, 1)
    step = 2
    while step < count:
        mine = mine + exchange(mine, step)
        step *= 2
    return mine, exchange(mine, 1)


def body(
    biomass,
    enzymes,
    substrates,
    monomers,
    enz_traits,
    mono_traits,
    enz_target,
    prod_rate,
    uptake_rate,
    mortality,
    disperse,
    enz_loss,
    vmax,
    kmich,
    khalf,
    offsets,
):
    ring = lax.axis_size("space")
    forward = [(i, (i + 1) % ring) for i in range(ring)]
    backward = [(target, source) for source, target in forward]

    def down(x):
        return lax.ppermute(x, "space", forward)

    def up(x):
        return lax.ppermute(x, "space", backward)

    count, rows, width = biomass.shape
    block = min(count, 256)

    first, last = take_rows(biomass, (0, 1, rows - 2, rows - 1))
    inner_low, inner_high = down(last), up(first)
    middle = take_rows(biomass, tuple(range(2, rows - 2)))
    row_pairs = [first, *middle, last]

    enz_f = enz_traits.astype(F32)
    mono_f = mono_traits.astype(F32)
    weight = jnp.concatenate(
        [
            enz_f * prod_rate[:, None],
            mono_f * uptake_rate[:, None],
            jnp.zeros((count, PADDED - enz_f.shape[1] - mono_f.shape[1]), F32),
        ],
        1,
    ).T
    weights = jnp.concatenate(pieces_outside(weight, 2), 0)
    keep = 1.0 - mortality - prod_rate * jnp.sum(enz_f, axis=1)
    gain = jnp.concatenate(
        [
            (YIELD * uptake_rate)[:, None] * mono_f,
            keep[:, None],
            jnp.zeros((count, SLOTS - 1 - mono_f.shape[1]), F32),
        ],
        1,
    )
    gain = trait_operand(gain)
    fraction = jnp.broadcast_to((disperse / KOFF)[:, None], (count, HALF))
    circulant = circulants(offsets, width)
    cells = (enz_loss, vmax, kmich, khalf, enz_target)

    odd = lax.rem(lax.axis_index("taxa"), 2).reshape(1).astype(jnp.int32)

    sums = over_taxa(*taxa_sums(row_pairs, weights, odd, block))
    enzymes, substrates, monomers, share_one = cell_update(*sums, odd, enzymes, substrates, monomers, *cells)
    share_low, share_high = down(share_one[rows - 4 :]), up(share_one[:4])
    spreading = (gain, fraction, circulant)
    inside, inside_sums = day_one_inside(row_pairs, share_one, *spreading, weights, block)

    inner_low, inner_high, share_low, share_high, inside, outer_first, outer_last = lax.optimization_barrier(
        (inner_low, inner_high, share_low, share_high, inside, middle[0], middle[-1])
    )
    outer_low, outer_high = down(outer_last), up(outer_first)

    def rest_of_day_one(low, high, share_low, share_high, enzymes, substrates, monomers):
        rim, *sums = day_one_rim(
            low, high, inside, inside_sums, share_low, share_high, *spreading, weights, odd, block
        )
        sums = over_taxa(*sums)
        return rim, *cell_update(*sums, odd, enzymes, substrates, monomers, *cells)

    def unused(*operands):
        shapes = jax.eval_shape(rest_of_day_one, *operands)
        return jax.tree.map(lambda x: jnp.zeros(x.shape, x.dtype), shapes)

    rim, enzymes, substrates, monomers, share_two = lax.cond(
        offsets[0, 0] < 3,
        rest_of_day_one,
        unused,
        inner_low,
        inner_high,
        share_low,
        share_high,
        enzymes,
        substrates,
        monomers,
    )
    near_low, near_high = down(share_two[rows - 2 :]), up(share_two[:2])
    beyond = day_one_beyond(
        row_pairs, inner_low, inner_high, share_one, share_low, share_high, *spreading, block
    )
    biomass_out, edge = day_two(inside, rim, share_two, *spreading, block)
    biomass_out = edges(
        outer_low,
        outer_high,
        beyond,
        edge,
        biomass_out,
        jnp.concatenate([share_low[:2], share_high[2:]], 0),
        jnp.concatenate([near_low, near_high], 0),
        gain,
        fraction,
        circulant,
        block,
    )
    return (biomass_out, enzymes, substrates, monomers)


def solution(mesh):
    placed = (
        P("taxa", "space", None),
        P(None, "space", None),
        P(None, "space", None),
        P(None, "space", None),
        P("taxa", None),
        P("taxa", None),
        P(),
        P("taxa"),
        P("taxa"),
        P("taxa"),
        P("taxa"),
        P(),
        P(),
        P(),
        P(),
        P(),
    )
    return jax.shard_map(
        body,
        mesh=mesh,
        in_specs=placed,
        out_specs=(
            P("taxa", "space", None),
            P(None, "space", None),
            P(None, "space", None),
            P(None, "space", None),
        ),
        check_vma=False,
    )
```

```python
import jax
import jax.numpy as jnp
from jax import lax
from jax.experimental import pallas as pl
from jax.experimental.pallas import tpu as pltpu
from jax.sharding import PartitionSpec as P

KOFF = 8
YIELD = 0.6
HALF = 128
SLOTS = 16
CHAN = 56
PADDED = 64
F32 = jnp.float32
BF16 = jnp.bfloat16
ANY = pl.BlockSpec(memory_space=pl.ANY)
SMEM = pl.BlockSpec(memory_space=pltpu.SMEM)
VMEM_BYTES = 40 << 20


def params():
    return pltpu.CompilerParams(vmem_limit_bytes=VMEM_BYTES)


def cost(flops, moved):
    return pl.CostEstimate(flops=flops, bytes_accessed=moved, transcendentals=0)


def split(x, count):
    out = []
    for _ in range(count):
        part = x.astype(BF16)
        out.append(part)
        x = x - part.astype(F32)
    return out


def share_operand(share):
    high, mid, low = split(share, 3)
    return jnp.concatenate([high, mid, low, high, mid, high], 0)


def matmul(a, b):
    return jnp.dot(a, b, preferred_element_type=F32)


def take_first(biomass, rows, pieces):
    count, height, width = biomass.shape
    pairs = len(rows) // 2
    step = count // pieces

    def kernel(source, *refs):
        outs, held, arrived, left = refs[:pairs], refs[pairs], refs[pairs + 1], refs[pairs + 2]
        loads, stores = [], []
        for p in range(pieces):
            taxa = pl.ds(p * step, step)
            loads.append(pltpu.make_async_copy(source.at[taxa], held.at[taxa], arrived.at[p]))
            loads[-1].start()
        for p in range(pieces):
            taxa = pl.ds(p * step, step)
            loads[p].wait()
            for i, row in enumerate(rows):
                stores.append(
                    pltpu.make_async_copy(held.at[taxa, row, :], outs[i // 2].at[i % 2, taxa], left.at[p, i])
                )
                stores[-1].start()
        for copy in stores:
            copy.wait()

    return pl.pallas_call(
        kernel,
        name="take_first",
        out_shape=[jax.ShapeDtypeStruct((2, count, width), F32)] * pairs,
        in_specs=[ANY],
        out_specs=[ANY] * pairs,
        scratch_shapes=[
            pltpu.VMEM((count, height, width), F32),
            pltpu.SemaphoreType.DMA((pieces,)),
            pltpu.SemaphoreType.DMA((pieces, len(rows))),
        ],
        compiler_params=pltpu.CompilerParams(vmem_limit_bytes=60 << 20),
        cost_estimate=cost(1000, 1000),
    )(biomass)


def add_sums(total, row, x, weights):
    high, low = split(x, 2)
    first = matmul(weights, high)
    second = matmul(weights[:PADDED], low)
    total[row] += first[:PADDED] + first[PADDED:] + second


def finish_sums(total, odd, mine, other):
    low = jnp.swapaxes(total[:, : CHAN // 2, :], 0, 1)
    high = jnp.swapaxes(total[:, CHAN // 2 : CHAN, :], 0, 1)

    @pl.when(odd[0] == 0)
    def _():
        mine[...] = low
        other[...] = high

    @pl.when(odd[0] != 0)
    def _():
        mine[...] = high
        other[...] = low


def sum_weights(enz_traits, mono_traits, prod_rate, uptake_rate):
    n_enz, count = enz_traits.shape
    used = n_enz + mono_traits.shape[0]

    def kernel(enz, mono, prod, uptake, out, held):
        held[:n_enz] = enz[...].astype(F32) * prod[...]
        held[n_enz:used] = mono[...].astype(F32) * uptake[...]
        held[used:] = jnp.zeros((PADDED - used, count), F32)
        high, low = split(held[...], 2)
        out[:PADDED] = high
        out[PADDED:] = low

    return pl.pallas_call(
        kernel,
        name="sum_weights",
        out_shape=jax.ShapeDtypeStruct((2 * PADDED, count), BF16),
        scratch_shapes=[pltpu.VMEM((PADDED, count), F32)],
        compiler_params=params(),
        cost_estimate=cost(1000, 1000),
    )(enz_traits, mono_traits, prod_rate, uptake_rate)


def spread_operands(enz_traits, mono_traits, prod_rate, uptake_rate, mortality, disperse, offsets, width):
    count = enz_traits.shape[1]
    n_mono = mono_traits.shape[0]

    def kernel(enz, mono, prod, uptake, mort, disp, offs, gain, fraction, circulant, held, stacked):
        held[...] = jnp.zeros_like(held)
        held[:n_mono] = (YIELD * uptake[...]) * mono[...].astype(F32)
        made = jnp.sum(enz[...].astype(F32), axis=0, keepdims=True)
        held[n_mono : n_mono + 1] = 1.0 - mort[...] - prod[...] * made
        high, mid, low = (part.astype(F32) for part in split(held[...], 3))
        stacked[...] = jnp.zeros_like(stacked)
        for i, part in enumerate((high, high, high, mid, mid, low)):
            stacked[SLOTS * i : SLOTS * (i + 1)] = part
        gain[...] = stacked[...].T[:, : 6 * SLOTS].astype(BF16)
        fraction[...] = jnp.broadcast_to(disp[...] * (1.0 / KOFF), (HALF, count)).T
        source = lax.broadcasted_iota(jnp.int32, (width, width), 0)
        target = lax.broadcasted_iota(jnp.int32, (width, width), 1)
        apart = (target - source + width + 2) & (width - 1)
        for i in range(5):
            total = jnp.zeros((width, width), F32)
            for j in range(5):
                number = jnp.int32(-KOFF if i == 2 and j == 2 else 0)
                for k in range(KOFF):
                    hit = (offs[k, 0] == 2 - i) & (offs[k, 1] == j - 2)
                    number = number + hit.astype(jnp.int32)
                total = jnp.where(apart == j, number.astype(F32), total)
            circulant[width * i : width * (i + 1)] = total.astype(BF16)

    vmem = pl.BlockSpec(memory_space=pltpu.VMEM)
    return pl.pallas_call(
        kernel,
        name="spread_operands",
        out_shape=[
            jax.ShapeDtypeStruct((count, 6 * SLOTS), BF16),
            jax.ShapeDtypeStruct((count, HALF), F32),
            jax.ShapeDtypeStruct((5 * width, width), BF16),
        ],
        in_specs=[vmem] * 6 + [SMEM],
        out_specs=[vmem] * 3,
        scratch_shapes=[pltpu.VMEM((SLOTS, count), F32), pltpu.VMEM((HALF, count), F32)],
        compiler_params=params(),
        cost_estimate=cost(1000, 1000),
    )(enz_traits, mono_traits, prod_rate, uptake_rate, mortality, disperse, offsets)


def first_sums(biomass, weights, odd, block):
    count, rows, width = biomass.shape
    inner = rows // 2 - 2

    def kernel(source, weight, side, *refs):
        pairs, (mine, other, total) = refs[:inner], refs[inner:]

        @pl.when(pl.program_id(0) == 0)
        def _():
            total[...] = jnp.zeros_like(total)

        x = jnp.swapaxes(source[...], 0, 1)
        for row in range(rows):
            if 2 <= row < rows - 2:
                pairs[row // 2 - 1][row % 2] = x[row]
            add_sums(total, row, x[row], weight[...])

        @pl.when(pl.program_id(0) == pl.num_programs(0) - 1)
        def _():
            finish_sums(total, side, mine, other)

    half = (CHAN // 2, rows, width)
    return pl.pallas_call(
        kernel,
        name="first_sums",
        grid=(count // block,),
        out_shape=[jax.ShapeDtypeStruct((2, count, width), F32)] * inner + [jax.ShapeDtypeStruct(half, F32)] * 2,
        in_specs=[
            pl.BlockSpec((block, rows, width), lambda i: (i, 0, 0)),
            pl.BlockSpec((2 * PADDED, block), lambda i: (0, i)),
            SMEM,
        ],
        out_specs=[pair_spec(block, width)] * inner + [whole(half)] * 2,
        scratch_shapes=[pltpu.VMEM((rows, PADDED, width), F32)],
        compiler_params=params(),
        cost_estimate=cost(1000, 1000),
    )(biomass, weights, odd)


def cell_update(mine, rest, odd, enz, sub, mono, enz_loss, vmax, kmich, khalf, enz_target):
    n_enz, rows, width = enz.shape
    n_sub, n_mono = sub.shape[0], mono.shape[0]

    def kernel(*refs):
        mine, rest, enz, sub, mono, side, loss, vmax, kmich, khalf, target = refs[:11]
        pool, left, mono_two, out, sums, speed, rate, share = refs[11:]
        half = mine.shape[0]

        @pl.when(side[0] == 0)
        def _():
            sums[:half] = mine[...]
            sums[half:] = rest[...]

        @pl.when(side[0] != 0)
        def _():
            sums[:half] = rest[...]
            sums[half:] = mine[...]

        rate[...] = jnp.zeros_like(rate)
        for e in range(n_enz):
            now = enz[e] * (1.0 - loss[e]) + sums[e]
            pool[e] = now
            speed[e] = vmax[e] * now / (kmich[e] + sub[target[e]])
        for e in range(n_enz):
            rate[target[e]] += speed[e]

        def finish(m, mono_one):
            demand = sums[n_enz + m]
            part = mono_one / (khalf[m] + demand + mono_one)
            mono_two[m] = mono_one - demand * part
            share[m] = part

        for s in range(n_sub):
            kept = sub[s] * jnp.exp(-rate[s])
            left[s] = kept
            finish(s, mono[s] + (sub[s] - kept))
        for m in range(n_sub, n_mono):
            finish(m, mono[m])
        share[n_mono] = jnp.ones((rows, width), F32)
        for m in range(n_mono + 1, SLOTS):
            share[m] = jnp.zeros((rows, width), F32)
        out[...] = jnp.swapaxes(share[...], 0, 1)

    vmem = pl.BlockSpec(memory_space=pltpu.VMEM)
    return pl.pallas_call(
        kernel,
        name="cell_update",
        out_shape=[
            jax.ShapeDtypeStruct(enz.shape, F32),
            jax.ShapeDtypeStruct(sub.shape, F32),
            jax.ShapeDtypeStruct(mono.shape, F32),
            jax.ShapeDtypeStruct((rows, SLOTS, width), F32),
        ],
        in_specs=[vmem] * 5 + [SMEM] * 6,
        out_specs=[vmem] * 4,
        scratch_shapes=[
            pltpu.VMEM((CHAN, rows, width), F32),
            pltpu.VMEM(enz.shape, F32),
            pltpu.VMEM(sub.shape, F32),
            pltpu.VMEM((SLOTS, rows, width), F32),
        ],
        compiler_params=params(),
        cost_estimate=cost(1000, 1000),
    )(mine, rest, enz, sub, mono, odd, enz_loss, vmax, kmich, khalf, enz_target)


def store_pieces(pieces, index, value):
    count, width = value.shape
    columns = slice(width * index, width * (index + 1))
    high, low = split(value, 2)
    pieces[:count, columns] = high
    pieces[count:, columns] = low


def stencil(pieces, circulant, first, count, offset):
    width = circulant.shape[1]
    both = matmul(
        pieces[:, width * first : width * (first + count)],
        circulant[width * offset : width * (offset + count), :],
    )
    half = both.shape[0] // 2
    return both[:half] + both[half:]


def window(target, rows):
    first = max(target - 2, 0)
    return first, min(target + 2, rows - 1) - first + 1, first - target + 2


def spread(value, fraction, change):
    return value + jnp.concatenate([fraction, fraction], 1) * change


def whole(shape):
    return pl.BlockSpec(shape, lambda i: (0,) * len(shape))


def pair_spec(block, width, at=0):
    return pl.BlockSpec((2, block, width), lambda i: (at, i, 0))


def taxa_spec(block, width):
    return pl.BlockSpec((block, width), lambda i: (i, 0))


def day_one_inside(row_pairs, share, gain, fraction, circulant, weights, block):
    _, count, width = row_pairs[0].shape
    rows = 2 * len(row_pairs)
    inner = rows - 4

    def kernel(*refs):
        pairs = refs[: len(row_pairs)]
        own, gain_w, frac, circ, weight, out, to_next, to_previous, total, pieces = refs[len(row_pairs) :]

        @pl.when(pl.program_id(0) == 0)
        def _():
            total[...] = jnp.zeros_like(total)

        for row in range(rows):
            value = pairs[row // 2][row % 2] * matmul(gain_w[...], share_operand(own[row]))
            out[row] = value
            store_pieces(pieces, row, value)
        for row in range(rows):
            value = spread(out[row], frac[...], stencil(pieces, circ, *window(row, rows)))
            out[row] = value
            if 2 <= row < rows - 2:
                add_sums(total, row - 2, value, weight[...])
        for i, (source, number, offset) in enumerate(TERMS):
            source += rows - 4 if i < 2 else 0
            value = spread(0.0, frac[...], stencil(pieces, circ, source, number, offset))
            (to_next if i < 2 else to_previous)[i % 2] = value

    return pl.pallas_call(
        kernel,
        name="day_one_inside",
        grid=(count // block,),
        out_shape=[
            jax.ShapeDtypeStruct((rows, count, width), F32),
            *[jax.ShapeDtypeStruct((2, count, width), F32)] * 2,
            jax.ShapeDtypeStruct((inner, PADDED, width), F32),
        ],
        in_specs=[pair_spec(block, width)] * len(row_pairs)
        + [
            whole(share.shape),
            taxa_spec(block, gain.shape[1]),
            taxa_spec(block, HALF),
            whole(circulant.shape),
            pl.BlockSpec((2 * PADDED, block), lambda i: (0, i)),
        ],
        out_specs=[
            pl.BlockSpec((rows, block, width), lambda i: (0, i, 0)),
            pair_spec(block, width),
            pair_spec(block, width),
            whole((inner, PADDED, width)),
        ],
        scratch_shapes=[pltpu.VMEM((2 * block, rows * width), BF16)],
        compiler_params=params(),
        cost_estimate=cost(1000, 1000),
    )(*row_pairs, share, gain, fraction, circulant, weights)


TERMS = ((0, 2, 0), (1, 1, 0), (2, 1, 4), (2, 2, 3))


def day_one_rim(low, high, inside, sums, share_low, share_high, gain, fraction, circulant, weights, odd, block):
    _, count, width = low.shape
    rows = inside.shape[0]

    def kernel(
        low, high, first, last, part, before, after, gain_w, frac, circ, weight, side, out, mine, other, far, total
    ):
        @pl.when(pl.program_id(0) == 0)
        def _():
            total[2 : rows - 2] = part[...]
            for row in (0, 1, rows - 2, rows - 1):
                total[row] = jnp.zeros((PADDED, width), F32)

        for i in range(4):
            x = low[i] if i < 2 else high[i - 2]
            s = before[i] if i < 2 else after[i - 2]
            store_pieces(far, i, x * matmul(gain_w[...], share_operand(s)))
        for i in range(4):
            x = first[i] if i < 2 else last[i - 2]
            value = spread(x, frac[...], stencil(far, circ, *TERMS[i]))
            out[i] = value
            add_sums(total, i if i < 2 else rows - 4 + i, value, weight[...])

        @pl.when(pl.program_id(0) == pl.num_programs(0) - 1)
        def _():
            finish_sums(total, side, mine, other)

    half = (CHAN // 2, rows, width)
    return pl.pallas_call(
        kernel,
        name="day_one_rim",
        grid=(count // block,),
        out_shape=[jax.ShapeDtypeStruct((4, count, width), F32)] + [jax.ShapeDtypeStruct(half, F32)] * 2,
        in_specs=[
            pair_spec(block, width),
            pair_spec(block, width),
            pair_spec(block, width),
            pair_spec(block, width, rows // 2 - 1),
            whole(sums.shape),
            whole(share_low.shape),
            whole(share_high.shape),
            taxa_spec(block, gain.shape[1]),
            taxa_spec(block, HALF),
            whole(circulant.shape),
            pl.BlockSpec((2 * PADDED, block), lambda i: (0, i)),
            SMEM,
        ],
        out_specs=[pl.BlockSpec((4, block, width), lambda i: (0, i, 0))] + [whole(half)] * 2,
        scratch_shapes=[
            pltpu.VMEM((2 * block, 4 * width), BF16),
            pltpu.VMEM((rows, PADDED, width), F32),
        ],
        compiler_params=params(),
        cost_estimate=cost(1000, 1000),
    )(low, high, inside, inside, sums, share_low, share_high, gain, fraction, circulant, weights, odd)


def day_one_beyond(row_pairs, low, high, share, share_low, share_high, gain, fraction, circulant, block):
    _, count, width = low.shape
    rows = 2 * len(row_pairs)

    def kernel(low, high, first, last, own, before, after, gain_w, frac, circ, out, pieces):
        for side in range(2):
            for i in range(4):
                if side == 0:
                    x = low[i] if i < 2 else first[i - 2]
                    s = before[i] if i < 2 else own[i - 2]
                else:
                    x = last[i] if i < 2 else high[i - 2]
                    s = own[rows - 2 + i] if i < 2 else after[i - 2]
                value = x * matmul(gain_w[...], share_operand(s))
                store_pieces(pieces, i, value)
                if (i < 2) == (side == 0):
                    out[i] = value
            for i in (0, 1) if side == 0 else (2, 3):
                out[i] = spread(out[i], frac[...], stencil(pieces, circ, *window(i, 4)))

    return pl.pallas_call(
        kernel,
        name="day_one_beyond",
        grid=(count // block,),
        out_shape=jax.ShapeDtypeStruct((4, count, width), F32),
        in_specs=[pair_spec(block, width)] * 4
        + [
            whole(share.shape),
            whole(share_low.shape),
            whole(share_high.shape),
            taxa_spec(block, gain.shape[1]),
            taxa_spec(block, HALF),
            whole(circulant.shape),
        ],
        out_specs=pl.BlockSpec((4, block, width), lambda i: (0, i, 0)),
        scratch_shapes=[pltpu.VMEM((2 * block, 4 * width), BF16)],
        compiler_params=params(),
        cost_estimate=cost(1000, 1000),
    )(low, high, row_pairs[0], row_pairs[-1], share, share_low, share_high, gain, fraction, circulant)


def day_two(inside, rim, share, gain, fraction, circulant, block):
    rows, count, width = inside.shape
    steps = count // block
    middle = rows // 2 - 2

    def kernel(*refs):
        inner = refs[:middle]
        outer, own, gain_w, frac, circ, out, edge, pieces, result, sem = refs[middle:]
        step = pl.program_id(0)
        slot = lax.rem(step, 2)

        def copies(at, where):
            found = []
            taxa = pl.ds(pl.multiple_of(at * block, block), block)
            for row in range(rows):
                if 2 <= row < rows - 2:
                    target = out.at[taxa, row, :]
                else:
                    target = edge.at[row if row < 2 else row - rows + 4, taxa, :]
                found.append(pltpu.make_async_copy(result.at[where, row], target, sem.at[where, row]))
            return found

        @pl.when(step >= 2)
        def _():
            for copy in copies(step - 2, slot):
                copy.wait()

        for row in range(rows):
            if 2 <= row < rows - 2:
                x = inner[row // 2 - 1][row % 2]
            else:
                x = outer[row if row < 2 else row - rows + 4]
            value = x * matmul(gain_w[...], share_operand(own[row]))
            result[slot, row] = value
            store_pieces(pieces, row, value)
        for row in range(rows):
            result[slot, row] = spread(result[slot, row], frac[...], stencil(pieces, circ, *window(row, rows)))
        for copy in copies(step, slot):
            copy.start()

        @pl.when(step == steps - 1)
        def _():
            if steps > 1:
                for copy in copies(step - 1, 1 - slot):
                    copy.wait()
            for copy in copies(step, slot):
                copy.wait()

    return pl.pallas_call(
        kernel,
        name="day_two",
        grid=(steps,),
        out_shape=[
            jax.ShapeDtypeStruct((count, rows, width), F32),
            jax.ShapeDtypeStruct((4, count, width), F32),
        ],
        in_specs=[
            *[pair_spec(block, width, 1 + i) for i in range(middle)],
            pl.BlockSpec((4, block, width), lambda i: (0, i, 0)),
            whole(share.shape),
            taxa_spec(block, gain.shape[1]),
            taxa_spec(block, HALF),
            whole(circulant.shape),
        ],
        out_specs=[ANY, ANY],
        scratch_shapes=[
            pltpu.VMEM((2 * block, rows * width), BF16),
            pltpu.VMEM((2, rows, block, width), F32),
            pltpu.SemaphoreType.DMA((2, rows)),
        ],
        compiler_params=params(),
        cost_estimate=cost(1000, 1000),
    )(*[inside] * middle, rim, share, gain, fraction, circulant)


def edges(early_low, late_low, from_high, beyond, edge, biomass_out, share_low, share_high, gain, fraction, circulant, block):
    _, count, width = from_high.shape
    rows = biomass_out.shape[1]
    steps = count // block

    def kernel(
        early, late, high, near_low, near_high, own, before, after, gain_w, frac, circ, unused, out, near, result, sem
    ):
        step = pl.program_id(0)
        slot = lax.rem(step, 2)

        def copies(at, where):
            taxa = pl.ds(pl.multiple_of(at * block, block), block)
            return [
                pltpu.make_async_copy(
                    result.at[where, i],
                    out.at[taxa, i if i < 2 else rows - 4 + i, :],
                    sem.at[where, i],
                )
                for i in range(4)
            ]

        @pl.when(step >= 2)
        def _():
            for copy in copies(step - 2, slot):
                copy.wait()

        for i in range(4):
            if i < 2:
                value = near_low[i] + jnp.where(step == 0, early[i], late[i])
            else:
                value = near_high[i - 2] + high[i - 2]
            s = before[i] if i < 2 else after[i - 2]
            store_pieces(near, i, value * matmul(gain_w[...], share_operand(s)))
        for i in range(4):
            result[slot, i] = spread(own[i], frac[...], stencil(near, circ, *TERMS[i]))
        for copy in copies(step, slot):
            copy.start()

        @pl.when(step == steps - 1)
        def _():
            if steps > 1:
                for copy in copies(step - 1, 1 - slot):
                    copy.wait()
            for copy in copies(step, slot):
                copy.wait()

    return pl.pallas_call(
        kernel,
        name="edges",
        grid=(steps,),
        out_shape=jax.ShapeDtypeStruct(biomass_out.shape, F32),
        in_specs=[
            whole(early_low.shape),
            whole(late_low.shape),
            pair_spec(block, width),
            pl.BlockSpec((2, block, width), lambda i: (0, i, 0)),
            pl.BlockSpec((2, block, width), lambda i: (1, i, 0)),
            pl.BlockSpec((4, block, width), lambda i: (0, i, 0)),
            whole(share_low.shape),
            whole(share_high.shape),
            pl.BlockSpec((block, gain.shape[1]), lambda i: (i, 0)),
            pl.BlockSpec((block, HALF), lambda i: (i, 0)),
            whole(circulant.shape),
            ANY,
        ],
        out_specs=ANY,
        scratch_shapes=[
            pltpu.VMEM((2 * block, 4 * width), BF16),
            pltpu.VMEM((2, 4, block, width), F32),
            pltpu.SemaphoreType.DMA((2, 4)),
        ],
        input_output_aliases={11: 0},
        compiler_params=params(),
        cost_estimate=cost(1000, 1000),
    )(
        early_low,
        late_low,
        from_high,
        beyond,
        beyond,
        edge,
        share_low,
        share_high,
        gain,
        fraction,
        circulant,
        biomass_out,
    )


def over_taxa(mine, other):
    count = lax.axis_size("taxa")

    def exchange(x, step):
        return lax.ppermute(x, "taxa", [(i, i ^ step) for i in range(count)])

    mine = mine + exchange(other, 1)
    step = 2
    while step < count:
        mine = mine + exchange(mine, step)
        step *= 2
    return mine, exchange(mine, 1)


def as_branch(offsets, run, *operands):
    def unused(*operands):
        return jax.tree.map(lambda x: jnp.zeros(x.shape, x.dtype), jax.eval_shape(run, *operands))

    return lax.cond(offsets[0, 0] < 3, run, unused, *operands)


def body(
    biomass,
    enzymes,
    substrates,
    monomers,
    enz_traits,
    mono_traits,
    enz_target,
    prod_rate,
    uptake_rate,
    mortality,
    disperse,
    enz_loss,
    vmax,
    kmich,
    khalf,
    offsets,
):
    ring = lax.axis_size("space")
    forward = [(i, (i + 1) % ring) for i in range(ring)]
    backward = [(target, source) for source, target in forward]

    def down(x):
        return lax.ppermute(x, "space", forward)

    def up(x):
        return lax.ppermute(x, "space", backward)

    count, rows, width = biomass.shape
    block = min(count, 256)

    first, last = take_first(biomass, (0, 1, rows - 2, rows - 1), 4)
    inner_low, inner_high = down(last), up(first)
    odd = lax.rem(lax.axis_index("taxa"), 2).reshape(1).astype(jnp.int32)
    traits = (enz_traits.T, mono_traits.T, prod_rate.reshape(1, count), uptake_rate.reshape(1, count))
    cells = (enz_loss, vmax, kmich, khalf, enz_target)

    def sums_and_cells(biomass, enzymes, substrates, monomers):
        weights = sum_weights(*traits)
        *middle, mine, other = first_sums(biomass, weights, odd, block)
        sums = over_taxa(mine, other)
        return *middle, weights, *cell_update(*sums, odd, enzymes, substrates, monomers, *cells)

    *middle, weights, enzymes, substrates, monomers, share_one = as_branch(
        offsets, sums_and_cells, biomass, enzymes, substrates, monomers
    )
    row_pairs = [first, *middle, last]
    spreading = spread_operands(
        *traits, mortality.reshape(1, count), disperse.reshape(1, count), offsets, width
    )
    share_low, share_high = down(share_one[rows - 2 :]), up(share_one[:2])
    inside, to_next, to_previous, inside_sums = day_one_inside(row_pairs, share_one, *spreading, weights, block)

    early = count // 2
    inner_low, inner_high, share_low, share_high, inside, next_early, to_previous = lax.optimization_barrier(
        (inner_low, inner_high, share_low, share_high, inside, to_next[:, :early], to_previous)
    )
    from_low, from_high = down(next_early), up(to_previous)

    def rest_of_day_one(low, high, share_low, share_high, enzymes, substrates, monomers):
        rim, *sums = day_one_rim(
            low, high, inside, inside_sums, share_low, share_high, *spreading, weights, odd, block
        )
        sums = over_taxa(*sums)
        return rim, *cell_update(*sums, odd, enzymes, substrates, monomers, *cells)

    rim, enzymes, substrates, monomers, share_two = as_branch(
        offsets,
        rest_of_day_one,
        inner_low,
        inner_high,
        share_low,
        share_high,
        enzymes,
        substrates,
        monomers,
    )
    near_low, near_high = down(share_two[rows - 2 :]), up(share_two[:2])
    inner_low, inner_high, share_two = lax.optimization_barrier((inner_low, inner_high, share_two))
    beyond = day_one_beyond(
        row_pairs, inner_low, inner_high, share_one, share_low, share_high, *spreading, block
    )
    beyond, next_late = lax.optimization_barrier((beyond, to_next[:, early:]))
    late_low = down(next_late)
    biomass_out, edge = day_two(inside, rim, share_two, *spreading, block)
    biomass_out = edges(
        from_low, late_low, from_high, beyond, edge, biomass_out, near_low, near_high, *spreading, early
    )
    return (biomass_out, enzymes, substrates, monomers)


def solution(mesh):
    placed = (
        P("taxa", "space", None),
        P(None, "space", None),
        P(None, "space", None),
        P(None, "space", None),
        P("taxa", None),
        P("taxa", None),
        P(),
        P("taxa"),
        P("taxa"),
        P("taxa"),
        P("taxa"),
        P(),
        P(),
        P(),
        P(),
        P(),
    )
    return jax.shard_map(
        body,
        mesh=mesh,
        in_specs=placed,
        out_specs=(
            P("taxa", "space", None),
            P(None, "space", None),
            P(None, "space", None),
            P(None, "space", None),
        ),
        check_vma=False,
    )
```

```python
import jax
import jax.numpy as jnp
from jax import lax
from jax.experimental import pallas as pl
from jax.experimental.pallas import tpu as pltpu
from jax.sharding import PartitionSpec as P

KOFF = 8
YIELD = 0.6
HALF = 128
SLOTS = 16
CHAN = 56
PADDED = 64
F32 = jnp.float32
BF16 = jnp.bfloat16
ANY = pl.BlockSpec(memory_space=pl.ANY)
SMEM = pl.BlockSpec(memory_space=pltpu.SMEM)
VMEM_BYTES = 40 << 20


def params():
    return pltpu.CompilerParams(vmem_limit_bytes=VMEM_BYTES)


def cost(flops, moved):
    return pl.CostEstimate(flops=flops, bytes_accessed=moved, transcendentals=0)


def split(x, count):
    out = []
    for _ in range(count):
        part = x.astype(BF16)
        out.append(part)
        x = x - part.astype(F32)
    return out


def share_operand(share):
    high, mid, low = split(share, 3)
    return jnp.concatenate([high, mid, low, high, mid, high], 0)


def matmul(a, b):
    return jnp.dot(a, b, preferred_element_type=F32)


def take_first(biomass, pieces):
    count, height, width = biomass.shape
    half, step = count // 2, count // pieces

    def kernel(source, first, early, late, held, arrived, left):
        loads, stores = [], []
        for p in range(pieces):
            taxa = pl.ds(p * step, step)
            loads.append(pltpu.make_async_copy(source.at[taxa], held.at[taxa], arrived.at[p]))
            loads[-1].start()
        for p in range(pieces):
            loads[p].wait()
            at = p * step
            last = early if at < half else late
            for i, row in enumerate((0, 1, height - 2, height - 1)):
                target = first.at[i, pl.ds(at, step)] if i < 2 else last.at[i - 2, pl.ds(at % half, step)]
                stores.append(pltpu.make_async_copy(held.at[pl.ds(at, step), row, :], target, left.at[p, i]))
                stores[-1].start()
        for copy in stores:
            copy.wait()

    return pl.pallas_call(
        kernel,
        name="take_first",
        out_shape=[jax.ShapeDtypeStruct((2, n, width), F32) for n in (count, half, half)],
        in_specs=[ANY],
        out_specs=[ANY] * 3,
        scratch_shapes=[
            pltpu.VMEM((count, height, width), F32),
            pltpu.SemaphoreType.DMA((pieces,)),
            pltpu.SemaphoreType.DMA((pieces, 4)),
        ],
        compiler_params=pltpu.CompilerParams(vmem_limit_bytes=60 << 20),
        cost_estimate=cost(1000, 1000),
    )(biomass)


def add_sums(total, row, x, weights):
    high, low = split(x, 2)
    first = matmul(weights, high)
    second = matmul(weights[:PADDED], low)
    total[row] += first[:PADDED] + first[PADDED:] + second


def finish_sums(total, odd, mine, other):
    low = jnp.swapaxes(total[:, : CHAN // 2, :], 0, 1)
    high = jnp.swapaxes(total[:, CHAN // 2 : CHAN, :], 0, 1)

    @pl.when(odd[0] == 0)
    def _():
        mine[...] = low
        other[...] = high

    @pl.when(odd[0] != 0)
    def _():
        mine[...] = high
        other[...] = low


def sum_weights(enz_traits, mono_traits, prod_rate, uptake_rate):
    n_enz, count = enz_traits.shape
    used = n_enz + mono_traits.shape[0]

    def kernel(enz, mono, prod, uptake, out, held):
        held[:n_enz] = enz[...].astype(F32) * prod[...]
        held[n_enz:used] = mono[...].astype(F32) * uptake[...]
        held[used:] = jnp.zeros((PADDED - used, count), F32)
        high, low = split(held[...], 2)
        out[:PADDED] = high
        out[PADDED:] = low

    return pl.pallas_call(
        kernel,
        name="sum_weights",
        out_shape=jax.ShapeDtypeStruct((2 * PADDED, count), BF16),
        scratch_shapes=[pltpu.VMEM((PADDED, count), F32)],
        compiler_params=params(),
        cost_estimate=cost(1000, 1000),
    )(enz_traits, mono_traits, prod_rate, uptake_rate)


def spread_operands(enz_traits, mono_traits, prod_rate, uptake_rate, mortality, disperse, offsets, width):
    count = enz_traits.shape[1]
    n_mono = mono_traits.shape[0]

    def kernel(enz, mono, prod, uptake, mort, disp, offs, gain, fraction, circulant, held, stacked):
        held[...] = jnp.zeros_like(held)
        held[:n_mono] = (YIELD * uptake[...]) * mono[...].astype(F32)
        made = jnp.sum(enz[...].astype(F32), axis=0, keepdims=True)
        held[n_mono : n_mono + 1] = 1.0 - mort[...] - prod[...] * made
        high, mid, low = (part.astype(F32) for part in split(held[...], 3))
        stacked[...] = jnp.zeros_like(stacked)
        for i, part in enumerate((high, high, high, mid, mid, low)):
            stacked[SLOTS * i : SLOTS * (i + 1)] = part
        gain[...] = stacked[...].T[:, : 6 * SLOTS].astype(BF16)
        fraction[...] = jnp.broadcast_to(disp[...] * (1.0 / KOFF), (HALF, count)).T
        source = lax.broadcasted_iota(jnp.int32, (width, width), 0)
        target = lax.broadcasted_iota(jnp.int32, (width, width), 1)
        apart = (target - source + width + 2) & (width - 1)
        for i in range(5):
            total = jnp.zeros((width, width), F32)
            for j in range(5):
                number = jnp.int32(-KOFF if i == 2 and j == 2 else 0)
                for k in range(KOFF):
                    hit = (offs[k, 0] == 2 - i) & (offs[k, 1] == j - 2)
                    number = number + hit.astype(jnp.int32)
                total = jnp.where(apart == j, number.astype(F32), total)
            circulant[width * i : width * (i + 1)] = total.astype(BF16)

    vmem = pl.BlockSpec(memory_space=pltpu.VMEM)
    return pl.pallas_call(
        kernel,
        name="spread_operands",
        out_shape=[
            jax.ShapeDtypeStruct((count, 6 * SLOTS), BF16),
            jax.ShapeDtypeStruct((count, HALF), F32),
            jax.ShapeDtypeStruct((5 * width, width), BF16),
        ],
        in_specs=[vmem] * 6 + [SMEM],
        out_specs=[vmem] * 3,
        scratch_shapes=[pltpu.VMEM((SLOTS, count), F32), pltpu.VMEM((HALF, count), F32)],
        compiler_params=params(),
        cost_estimate=cost(1000, 1000),
    )(enz_traits, mono_traits, prod_rate, uptake_rate, mortality, disperse, offsets)


def first_sums(biomass, weights, odd, block):
    count, rows, width = biomass.shape
    inner = rows // 2 - 1

    def kernel(source, weight, side, *refs):
        pairs, (mine, other, total) = refs[:inner], refs[inner:]

        @pl.when(pl.program_id(0) == 0)
        def _():
            total[...] = jnp.zeros_like(total)

        x = jnp.swapaxes(source[...], 0, 1)
        for row in range(rows):
            if row >= 2:
                pairs[row // 2 - 1][row % 2] = x[row]
            add_sums(total, row, x[row], weight[...])

        @pl.when(pl.program_id(0) == pl.num_programs(0) - 1)
        def _():
            finish_sums(total, side, mine, other)

    half = (CHAN // 2, rows, width)
    return pl.pallas_call(
        kernel,
        name="first_sums",
        grid=(count // block,),
        out_shape=[jax.ShapeDtypeStruct((2, count, width), F32)] * inner + [jax.ShapeDtypeStruct(half, F32)] * 2,
        in_specs=[
            pl.BlockSpec((block, rows, width), lambda i: (i, 0, 0)),
            pl.BlockSpec((2 * PADDED, block), lambda i: (0, i)),
            SMEM,
        ],
        out_specs=[pair_spec(block, width)] * inner + [whole(half)] * 2,
        scratch_shapes=[pltpu.VMEM((rows, PADDED, width), F32)],
        compiler_params=params(),
        cost_estimate=cost(1000, 1000),
    )(biomass, weights, odd)


def cell_update(mine, rest, odd, enz, sub, mono, enz_loss, vmax, kmich, khalf, enz_target):
    n_enz, rows, width = enz.shape
    n_sub, n_mono = sub.shape[0], mono.shape[0]

    def kernel(*refs):
        mine, rest, enz, sub, mono, side, loss, vmax, kmich, khalf, target = refs[:11]
        pool, left, mono_two, out, sums, speed, rate, share = refs[11:]
        half = mine.shape[0]

        @pl.when(side[0] == 0)
        def _():
            sums[:half] = mine[...]
            sums[half:] = rest[...]

        @pl.when(side[0] != 0)
        def _():
            sums[:half] = rest[...]
            sums[half:] = mine[...]

        rate[...] = jnp.zeros_like(rate)
        for e in range(n_enz):
            now = enz[e] * (1.0 - loss[e]) + sums[e]
            pool[e] = now
            speed[e] = vmax[e] * now / (kmich[e] + sub[target[e]])
        for e in range(n_enz):
            rate[target[e]] += speed[e]

        def finish(m, mono_one):
            demand = sums[n_enz + m]
            part = mono_one / (khalf[m] + demand + mono_one)
            mono_two[m] = mono_one - demand * part
            share[m] = part

        for s in range(n_sub):
            kept = sub[s] * jnp.exp(-rate[s])
            left[s] = kept
            finish(s, mono[s] + (sub[s] - kept))
        for m in range(n_sub, n_mono):
            finish(m, mono[m])
        share[n_mono] = jnp.ones((rows, width), F32)
        for m in range(n_mono + 1, SLOTS):
            share[m] = jnp.zeros((rows, width), F32)
        out[...] = jnp.swapaxes(share[...], 0, 1)

    vmem = pl.BlockSpec(memory_space=pltpu.VMEM)
    return pl.pallas_call(
        kernel,
        name="cell_update",
        out_shape=[
            jax.ShapeDtypeStruct(enz.shape, F32),
            jax.ShapeDtypeStruct(sub.shape, F32),
            jax.ShapeDtypeStruct(mono.shape, F32),
            jax.ShapeDtypeStruct((rows, SLOTS, width), F32),
        ],
        in_specs=[vmem] * 5 + [SMEM] * 6,
        out_specs=[vmem] * 4,
        scratch_shapes=[
            pltpu.VMEM((CHAN, rows, width), F32),
            pltpu.VMEM(enz.shape, F32),
            pltpu.VMEM(sub.shape, F32),
            pltpu.VMEM((SLOTS, rows, width), F32),
        ],
        compiler_params=params(),
        cost_estimate=cost(1000, 1000),
    )(mine, rest, enz, sub, mono, odd, enz_loss, vmax, kmich, khalf, enz_target)


def store_pieces(pieces, index, value):
    count, width = value.shape
    columns = slice(width * index, width * (index + 1))
    high, low = split(value, 2)
    pieces[:count, columns] = high
    pieces[count:, columns] = low


def stencil(pieces, circulant, first, count, offset):
    width = circulant.shape[1]
    both = matmul(
        pieces[:, width * first : width * (first + count)],
        circulant[width * offset : width * (offset + count), :],
    )
    half = both.shape[0] // 2
    return both[:half] + both[half:]


def window(target, rows):
    first = max(target - 2, 0)
    return first, min(target + 2, rows - 1) - first + 1, first - target + 2


def spread(value, fraction, change):
    return value + jnp.concatenate([fraction, fraction], 1) * change


def whole(shape):
    return pl.BlockSpec(shape, lambda i: (0,) * len(shape))


def pair_spec(block, width, at=0):
    return pl.BlockSpec((2, block, width), lambda i: (at, i, 0))


def taxa_spec(block, width):
    return pl.BlockSpec((block, width), lambda i: (i, 0))


def day_one_inside(row_pairs, share, gain, fraction, circulant, weights, block):
    _, count, width = row_pairs[0].shape
    rows = 2 * len(row_pairs)
    inner = rows - 4

    def kernel(*refs):
        pairs = refs[: len(row_pairs)]
        own, gain_w, frac, circ, weight, out, to_next, to_previous, total, pieces = refs[len(row_pairs) :]

        @pl.when(pl.program_id(0) == 0)
        def _():
            total[...] = jnp.zeros_like(total)

        for row in range(rows):
            value = pairs[row // 2][row % 2] * matmul(gain_w[...], share_operand(own[row]))
            out[row] = value
            store_pieces(pieces, row, value)
        for row in range(rows):
            value = spread(out[row], frac[...], stencil(pieces, circ, *window(row, rows)))
            out[row] = value
            if 2 <= row < rows - 2:
                add_sums(total, row - 2, value, weight[...])
        for i, (source, number, offset) in enumerate(TERMS):
            source += rows - 4 if i < 2 else 0
            value = spread(0.0, frac[...], stencil(pieces, circ, source, number, offset))
            (to_next if i < 2 else to_previous)[i % 2] = value

    return pl.pallas_call(
        kernel,
        name="day_one_inside",
        grid=(count // block,),
        out_shape=[
            jax.ShapeDtypeStruct((rows, count, width), F32),
            *[jax.ShapeDtypeStruct((2, count, width), F32)] * 2,
            jax.ShapeDtypeStruct((inner, PADDED, width), F32),
        ],
        in_specs=[pair_spec(block, width)] * len(row_pairs)
        + [
            whole(share.shape),
            taxa_spec(block, gain.shape[1]),
            taxa_spec(block, HALF),
            whole(circulant.shape),
            pl.BlockSpec((2 * PADDED, block), lambda i: (0, i)),
        ],
        out_specs=[
            pl.BlockSpec((rows, block, width), lambda i: (0, i, 0)),
            pair_spec(block, width),
            pair_spec(block, width),
            whole((inner, PADDED, width)),
        ],
        scratch_shapes=[pltpu.VMEM((2 * block, rows * width), BF16)],
        compiler_params=params(),
        cost_estimate=cost(1000, 1000),
    )(*row_pairs, share, gain, fraction, circulant, weights)


TERMS = ((0, 2, 0), (1, 1, 0), (2, 1, 4), (2, 2, 3))


def chosen(early, late):
    return jnp.where(pl.program_id(0) == 0, early, late)


def day_one_rim(early_low, late_low, high, inside, sums, share_low, share_high, gain, fraction, circulant, weights, odd, block):
    _, count, width = high.shape
    rows = inside.shape[0]

    def kernel(
        early, late, high, first, last, part, before, after, gain_w, frac, circ, weight, side, out, mine, other, far, total
    ):
        @pl.when(pl.program_id(0) == 0)
        def _():
            total[2 : rows - 2] = part[...]
            for row in (0, 1, rows - 2, rows - 1):
                total[row] = jnp.zeros((PADDED, width), F32)

        for i in range(4):
            x = chosen(early[i], late[i]) if i < 2 else high[i - 2]
            s = before[i] if i < 2 else after[i - 2]
            store_pieces(far, i, x * matmul(gain_w[...], share_operand(s)))
        for i in range(4):
            x = first[i] if i < 2 else last[i - 2]
            value = spread(x, frac[...], stencil(far, circ, *TERMS[i]))
            out[i] = value
            add_sums(total, i if i < 2 else rows - 4 + i, value, weight[...])

        @pl.when(pl.program_id(0) == pl.num_programs(0) - 1)
        def _():
            finish_sums(total, side, mine, other)

    half = (CHAN // 2, rows, width)
    return pl.pallas_call(
        kernel,
        name="day_one_rim",
        grid=(count // block,),
        out_shape=[jax.ShapeDtypeStruct((4, count, width), F32)] + [jax.ShapeDtypeStruct(half, F32)] * 2,
        in_specs=[
            whole(early_low.shape),
            whole(late_low.shape),
            pair_spec(block, width),
            pair_spec(block, width),
            pair_spec(block, width, rows // 2 - 1),
            whole(sums.shape),
            whole(share_low.shape),
            whole(share_high.shape),
            taxa_spec(block, gain.shape[1]),
            taxa_spec(block, HALF),
            whole(circulant.shape),
            pl.BlockSpec((2 * PADDED, block), lambda i: (0, i)),
            SMEM,
        ],
        out_specs=[pl.BlockSpec((4, block, width), lambda i: (0, i, 0))] + [whole(half)] * 2,
        scratch_shapes=[
            pltpu.VMEM((2 * block, 4 * width), BF16),
            pltpu.VMEM((rows, PADDED, width), F32),
        ],
        compiler_params=params(),
        cost_estimate=cost(1000, 1000),
    )(early_low, late_low, high, inside, inside, sums, share_low, share_high, gain, fraction, circulant, weights, odd)


def day_one_beyond(row_pairs, early_low, late_low, high, share, share_low, share_high, gain, fraction, circulant, block):
    _, count, width = high.shape
    rows = 2 * len(row_pairs)

    def kernel(early, late, high, first, last, own, before, after, gain_w, frac, circ, out, pieces):
        for side in range(2):
            for i in range(4):
                if side == 0:
                    x = chosen(early[i], late[i]) if i < 2 else first[i - 2]
                    s = before[i] if i < 2 else own[i - 2]
                else:
                    x = last[i] if i < 2 else high[i - 2]
                    s = own[rows - 2 + i] if i < 2 else after[i - 2]
                value = x * matmul(gain_w[...], share_operand(s))
                store_pieces(pieces, i, value)
                if (i < 2) == (side == 0):
                    out[i] = value
            for i in (0, 1) if side == 0 else (2, 3):
                out[i] = spread(out[i], frac[...], stencil(pieces, circ, *window(i, 4)))

    return pl.pallas_call(
        kernel,
        name="day_one_beyond",
        grid=(count // block,),
        out_shape=jax.ShapeDtypeStruct((4, count, width), F32),
        in_specs=[whole(early_low.shape), whole(late_low.shape)]
        + [pair_spec(block, width)] * 3
        + [
            whole(share.shape),
            whole(share_low.shape),
            whole(share_high.shape),
            taxa_spec(block, gain.shape[1]),
            taxa_spec(block, HALF),
            whole(circulant.shape),
        ],
        out_specs=pl.BlockSpec((4, block, width), lambda i: (0, i, 0)),
        scratch_shapes=[pltpu.VMEM((2 * block, 4 * width), BF16)],
        compiler_params=params(),
        cost_estimate=cost(1000, 1000),
    )(early_low, late_low, high, row_pairs[0], row_pairs[-1], share, share_low, share_high, gain, fraction, circulant)


def day_two(inside, rim, share, gain, fraction, circulant, block):
    rows, count, width = inside.shape
    steps = count // block
    middle = rows // 2 - 2

    def kernel(*refs):
        inner = refs[:middle]
        outer, own, gain_w, frac, circ, out, edge, pieces, result, sem = refs[middle:]
        step = pl.program_id(0)
        slot = lax.rem(step, 2)

        def copies(at, where):
            found = []
            taxa = pl.ds(pl.multiple_of(at * block, block), block)
            for row in range(rows):
                if 2 <= row < rows - 2:
                    target = out.at[taxa, row, :]
                else:
                    target = edge.at[row if row < 2 else row - rows + 4, taxa, :]
                found.append(pltpu.make_async_copy(result.at[where, row], target, sem.at[where, row]))
            return found

        @pl.when(step >= 2)
        def _():
            for copy in copies(step - 2, slot):
                copy.wait()

        for row in range(rows):
            if 2 <= row < rows - 2:
                x = inner[row // 2 - 1][row % 2]
            else:
                x = outer[row if row < 2 else row - rows + 4]
            value = x * matmul(gain_w[...], share_operand(own[row]))
            result[slot, row] = value
            store_pieces(pieces, row, value)
        for row in range(rows):
            result[slot, row] = spread(result[slot, row], frac[...], stencil(pieces, circ, *window(row, rows)))
        for copy in copies(step, slot):
            copy.start()

        @pl.when(step == steps - 1)
        def _():
            if steps > 1:
                for copy in copies(step - 1, 1 - slot):
                    copy.wait()
            for copy in copies(step, slot):
                copy.wait()

    return pl.pallas_call(
        kernel,
        name="day_two",
        grid=(steps,),
        out_shape=[
            jax.ShapeDtypeStruct((count, rows, width), F32),
            jax.ShapeDtypeStruct((4, count, width), F32),
        ],
        in_specs=[
            *[pair_spec(block, width, 1 + i) for i in range(middle)],
            pl.BlockSpec((4, block, width), lambda i: (0, i, 0)),
            whole(share.shape),
            taxa_spec(block, gain.shape[1]),
            taxa_spec(block, HALF),
            whole(circulant.shape),
        ],
        out_specs=[ANY, ANY],
        scratch_shapes=[
            pltpu.VMEM((2 * block, rows * width), BF16),
            pltpu.VMEM((2, rows, block, width), F32),
            pltpu.SemaphoreType.DMA((2, rows)),
        ],
        compiler_params=params(),
        cost_estimate=cost(1000, 1000),
    )(*[inside] * middle, rim, share, gain, fraction, circulant)


def edges(early_low, late_low, from_high, beyond, edge, biomass_out, share_low, share_high, gain, fraction, circulant, block):
    _, count, width = from_high.shape
    rows = biomass_out.shape[1]
    steps = count // block

    def kernel(
        early, late, high, near_low, near_high, own, before, after, gain_w, frac, circ, unused, out, near, result, sem
    ):
        step = pl.program_id(0)
        slot = lax.rem(step, 2)

        def copies(at, where):
            taxa = pl.ds(pl.multiple_of(at * block, block), block)
            return [
                pltpu.make_async_copy(
                    result.at[where, i],
                    out.at[taxa, i if i < 2 else rows - 4 + i, :],
                    sem.at[where, i],
                )
                for i in range(4)
            ]

        @pl.when(step >= 2)
        def _():
            for copy in copies(step - 2, slot):
                copy.wait()

        for i in range(4):
            if i < 2:
                value = near_low[i] + chosen(early[i], late[i])
            else:
                value = near_high[i - 2] + high[i - 2]
            s = before[i] if i < 2 else after[i - 2]
            store_pieces(near, i, value * matmul(gain_w[...], share_operand(s)))
        for i in range(4):
            result[slot, i] = spread(own[i], frac[...], stencil(near, circ, *TERMS[i]))
        for copy in copies(step, slot):
            copy.start()

        @pl.when(step == steps - 1)
        def _():
            if steps > 1:
                for copy in copies(step - 1, 1 - slot):
                    copy.wait()
            for copy in copies(step, slot):
                copy.wait()

    return pl.pallas_call(
        kernel,
        name="edges",
        grid=(steps,),
        out_shape=jax.ShapeDtypeStruct(biomass_out.shape, F32),
        in_specs=[
            whole(early_low.shape),
            whole(late_low.shape),
            pair_spec(block, width),
            pl.BlockSpec((2, block, width), lambda i: (0, i, 0)),
            pl.BlockSpec((2, block, width), lambda i: (1, i, 0)),
            pl.BlockSpec((4, block, width), lambda i: (0, i, 0)),
            whole(share_low.shape),
            whole(share_high.shape),
            pl.BlockSpec((block, gain.shape[1]), lambda i: (i, 0)),
            pl.BlockSpec((block, HALF), lambda i: (i, 0)),
            whole(circulant.shape),
            ANY,
        ],
        out_specs=ANY,
        scratch_shapes=[
            pltpu.VMEM((2 * block, 4 * width), BF16),
            pltpu.VMEM((2, 4, block, width), F32),
            pltpu.SemaphoreType.DMA((2, 4)),
        ],
        input_output_aliases={11: 0},
        compiler_params=params(),
        cost_estimate=cost(1000, 1000),
    )(
        early_low,
        late_low,
        from_high,
        beyond,
        beyond,
        edge,
        share_low,
        share_high,
        gain,
        fraction,
        circulant,
        biomass_out,
    )


def over_taxa(mine, other):
    count = lax.axis_size("taxa")

    def exchange(x, step):
        return lax.ppermute(x, "taxa", [(i, i ^ step) for i in range(count)])

    mine = mine + exchange(other, 1)
    step = 2
    while step < count:
        mine = mine + exchange(mine, step)
        step *= 2
    return mine, exchange(mine, 1)


def as_branch(offsets, run, *operands):
    def unused(*operands):
        return jax.tree.map(lambda x: jnp.zeros(x.shape, x.dtype), jax.eval_shape(run, *operands))

    return lax.cond(offsets[0, 0] < 3, run, unused, *operands)


def body(
    biomass,
    enzymes,
    substrates,
    monomers,
    enz_traits,
    mono_traits,
    enz_target,
    prod_rate,
    uptake_rate,
    mortality,
    disperse,
    enz_loss,
    vmax,
    kmich,
    khalf,
    offsets,
):
    ring = lax.axis_size("space")
    forward = [(i, (i + 1) % ring) for i in range(ring)]
    backward = [(target, source) for source, target in forward]

    def down(x):
        return lax.ppermute(x, "space", forward)

    def up(x):
        return lax.ppermute(x, "space", backward)

    count, rows, width = biomass.shape
    block = early = count // 2

    first, last_early, last_late = take_first(biomass, 4)
    inner_early, inner_high = down(last_early), up(first)
    odd = lax.rem(lax.axis_index("taxa"), 2).reshape(1).astype(jnp.int32)
    traits = (enz_traits.T, mono_traits.T, prod_rate.reshape(1, count), uptake_rate.reshape(1, count))
    cells = (enz_loss, vmax, kmich, khalf, enz_target)

    def sums_and_cells(biomass, enzymes, substrates, monomers):
        weights = sum_weights(*traits)
        *others, mine, other = first_sums(biomass, weights, odd, block)
        sums = over_taxa(mine, other)
        return *others, weights, *cell_update(*sums, odd, enzymes, substrates, monomers, *cells)

    *others, weights, enzymes, substrates, monomers, share_one = as_branch(
        offsets, sums_and_cells, biomass, enzymes, substrates, monomers
    )
    row_pairs = [first, *others]
    spreading = spread_operands(
        *traits, mortality.reshape(1, count), disperse.reshape(1, count), offsets, width
    )
    share_one, last_late = lax.optimization_barrier((share_one, last_late))
    share_low, share_high = down(share_one[rows - 2 :]), up(share_one[:2])
    inner_late = down(last_late)
    inside, to_next, to_previous, inside_sums = day_one_inside(row_pairs, share_one, *spreading, weights, block)

    inner_early, inner_late, inner_high, share_low, share_high, inside, next_early, to_previous = lax.optimization_barrier(
        (inner_early, inner_late, inner_high, share_low, share_high, inside, to_next[:, :early], to_previous)
    )
    from_low, from_high = down(next_early), up(to_previous)

    def rest_of_day_one(low_early, low_late, high, share_low, share_high, enzymes, substrates, monomers):
        rim, *sums = day_one_rim(
            low_early, low_late, high, inside, inside_sums, share_low, share_high, *spreading, weights, odd, block
        )
        sums = over_taxa(*sums)
        return rim, *cell_update(*sums, odd, enzymes, substrates, monomers, *cells)

    rim, enzymes, substrates, monomers, share_two = as_branch(
        offsets,
        rest_of_day_one,
        inner_early,
        inner_late,
        inner_high,
        share_low,
        share_high,
        enzymes,
        substrates,
        monomers,
    )
    near_low, near_high = down(share_two[rows - 2 :]), up(share_two[:2])
    inner_early, inner_high, share_two = lax.optimization_barrier((inner_early, inner_high, share_two))
    beyond = day_one_beyond(
        row_pairs, inner_early, inner_late, inner_high, share_one, share_low, share_high, *spreading, block
    )
    beyond, next_late = lax.optimization_barrier((beyond, to_next[:, early:]))
    late_low = down(next_late)
    biomass_out, edge = day_two(inside, rim, share_two, *spreading, block)
    biomass_out = edges(
        from_low, late_low, from_high, beyond, edge, biomass_out, near_low, near_high, *spreading, early
    )
    return (biomass_out, enzymes, substrates, monomers)


def solution(mesh):
    placed = (
        P("taxa", "space", None),
        P(None, "space", None),
        P(None, "space", None),
        P(None, "space", None),
        P("taxa", None),
        P("taxa", None),
        P(),
        P("taxa"),
        P("taxa"),
        P("taxa"),
        P("taxa"),
        P(),
        P(),
        P(),
        P(),
        P(),
    )
    return jax.shard_map(
        body,
        mesh=mesh,
        in_specs=placed,
        out_specs=(
            P("taxa", "space", None),
            P(None, "space", None),
            P(None, "space", None),
            P(None, "space", None),
        ),
        check_vma=False,
    )
```

```python
import jax
import jax.numpy as jnp
from jax import lax
from jax.experimental import pallas as pl
from jax.experimental.pallas import tpu as pltpu
from jax.sharding import PartitionSpec as P

KOFF = 8
YIELD = 0.6
HALF = 128
SLOTS = 16
CHAN = 56
PADDED = 64
F32 = jnp.float32
BF16 = jnp.bfloat16
ANY = pl.BlockSpec(memory_space=pl.ANY)
SMEM = pl.BlockSpec(memory_space=pltpu.SMEM)
VMEM_BYTES = 40 << 20


def params():
    return pltpu.CompilerParams(vmem_limit_bytes=VMEM_BYTES)


def cost(flops, moved):
    return pl.CostEstimate(flops=flops, bytes_accessed=moved, transcendentals=0)


def split(x, count):
    out = []
    for _ in range(count):
        part = x.astype(BF16)
        out.append(part)
        x = x - part.astype(F32)
    return out


def share_operand(share):
    high, mid, low = split(share, 3)
    return jnp.concatenate([high, mid, low, high, mid, high], 0)


def matmul(a, b):
    return jnp.dot(a, b, preferred_element_type=F32)


def take_first(biomass, rows, pieces):
    count, height, width = biomass.shape
    pairs = len(rows) // 2
    step = count // pieces

    def kernel(source, *refs):
        outs, held, arrived, left = refs[:pairs], refs[pairs], refs[pairs + 1], refs[pairs + 2]
        loads, stores = [], []
        for p in range(pieces):
            taxa = pl.ds(p * step, step)
            loads.append(pltpu.make_async_copy(source.at[taxa], held.at[taxa], arrived.at[p]))
            loads[-1].start()
        for p in range(pieces):
            taxa = pl.ds(p * step, step)
            loads[p].wait()
            for i, row in enumerate(rows):
                stores.append(
                    pltpu.make_async_copy(held.at[taxa, row, :], outs[i // 2].at[i % 2, taxa], left.at[p, i])
                )
                stores[-1].start()
        for copy in stores:
            copy.wait()

    return pl.pallas_call(
        kernel,
        name="take_first",
        out_shape=[jax.ShapeDtypeStruct((2, count, width), F32)] * pairs,
        in_specs=[ANY],
        out_specs=[ANY] * pairs,
        scratch_shapes=[
            pltpu.VMEM((count, height, width), F32),
            pltpu.SemaphoreType.DMA((pieces,)),
            pltpu.SemaphoreType.DMA((pieces, len(rows))),
        ],
        compiler_params=pltpu.CompilerParams(vmem_limit_bytes=60 << 20),
        cost_estimate=cost(1000, 1000),
    )(biomass)


def add_sums(total, row, x, weights):
    high, low = split(x, 2)
    first = matmul(weights, high)
    second = matmul(weights[:PADDED], low)
    total[row] += first[:PADDED] + first[PADDED:] + second


def finish_sums(total, odd, mine, other):
    low = jnp.swapaxes(total[:, : CHAN // 2, :], 0, 1)
    high = jnp.swapaxes(total[:, CHAN // 2 : CHAN, :], 0, 1)

    @pl.when(odd[0] == 0)
    def _():
        mine[...] = low
        other[...] = high

    @pl.when(odd[0] != 0)
    def _():
        mine[...] = high
        other[...] = low


def sum_weights(enz_traits, mono_traits, prod_rate, uptake_rate):
    n_enz, count = enz_traits.shape
    used = n_enz + mono_traits.shape[0]

    def kernel(enz, mono, prod, uptake, out, held):
        held[:n_enz] = enz[...].astype(F32) * prod[...]
        held[n_enz:used] = mono[...].astype(F32) * uptake[...]
        held[used:] = jnp.zeros((PADDED - used, count), F32)
        high, low = split(held[...], 2)
        out[:PADDED] = high
        out[PADDED:] = low

    return pl.pallas_call(
        kernel,
        name="sum_weights",
        out_shape=jax.ShapeDtypeStruct((2 * PADDED, count), BF16),
        scratch_shapes=[pltpu.VMEM((PADDED, count), F32)],
        compiler_params=params(),
        cost_estimate=cost(1000, 1000),
    )(enz_traits, mono_traits, prod_rate, uptake_rate)


def spread_operands(enz_traits, mono_traits, prod_rate, uptake_rate, mortality, disperse, offsets, width):
    count = enz_traits.shape[1]
    n_mono = mono_traits.shape[0]

    def kernel(enz, mono, prod, uptake, mort, disp, offs, gain, fraction, circulant, held, stacked):
        held[...] = jnp.zeros_like(held)
        held[:n_mono] = (YIELD * uptake[...]) * mono[...].astype(F32)
        made = jnp.sum(enz[...].astype(F32), axis=0, keepdims=True)
        held[n_mono : n_mono + 1] = 1.0 - mort[...] - prod[...] * made
        high, mid, low = (part.astype(F32) for part in split(held[...], 3))
        stacked[...] = jnp.zeros_like(stacked)
        for i, part in enumerate((high, high, high, mid, mid, low)):
            stacked[SLOTS * i : SLOTS * (i + 1)] = part
        gain[...] = stacked[...].T[:, : 6 * SLOTS].astype(BF16)
        fraction[...] = jnp.broadcast_to(disp[...] * (1.0 / KOFF), (HALF, count)).T
        source = lax.broadcasted_iota(jnp.int32, (width, width), 0)
        target = lax.broadcasted_iota(jnp.int32, (width, width), 1)
        apart = (target - source + width + 2) & (width - 1)
        for i in range(5):
            total = jnp.zeros((width, width), F32)
            for j in range(5):
                number = jnp.int32(-KOFF if i == 2 and j == 2 else 0)
                for k in range(KOFF):
                    hit = (offs[k, 0] == 2 - i) & (offs[k, 1] == j - 2)
                    number = number + hit.astype(jnp.int32)
                total = jnp.where(apart == j, number.astype(F32), total)
            circulant[width * i : width * (i + 1)] = total.astype(BF16)

    vmem = pl.BlockSpec(memory_space=pltpu.VMEM)
    return pl.pallas_call(
        kernel,
        name="spread_operands",
        out_shape=[
            jax.ShapeDtypeStruct((count, 6 * SLOTS), BF16),
            jax.ShapeDtypeStruct((count, HALF), F32),
            jax.ShapeDtypeStruct((5 * width, width), BF16),
        ],
        in_specs=[vmem] * 6 + [SMEM],
        out_specs=[vmem] * 3,
        scratch_shapes=[pltpu.VMEM((SLOTS, count), F32), pltpu.VMEM((HALF, count), F32)],
        compiler_params=params(),
        cost_estimate=cost(1000, 1000),
    )(enz_traits, mono_traits, prod_rate, uptake_rate, mortality, disperse, offsets)


def first_sums(biomass, weights, odd, block):
    count, rows, width = biomass.shape
    inner = rows // 2 - 2

    def kernel(source, weight, side, *refs):
        pairs, (mine, other, total) = refs[:inner], refs[inner:]

        @pl.when(pl.program_id(0) == 0)
        def _():
            total[...] = jnp.zeros_like(total)

        x = jnp.swapaxes(source[...], 0, 1)
        for row in range(rows):
            if 2 <= row < rows - 2:
                pairs[row // 2 - 1][row % 2] = x[row]
            add_sums(total, row, x[row], weight[...])

        @pl.when(pl.program_id(0) == pl.num_programs(0) - 1)
        def _():
            finish_sums(total, side, mine, other)

    half = (CHAN // 2, rows, width)
    return pl.pallas_call(
        kernel,
        name="first_sums",
        grid=(count // block,),
        out_shape=[jax.ShapeDtypeStruct((2, count, width), F32)] * inner + [jax.ShapeDtypeStruct(half, F32)] * 2,
        in_specs=[
            pl.BlockSpec((block, rows, width), lambda i: (i, 0, 0)),
            pl.BlockSpec((2 * PADDED, block), lambda i: (0, i)),
            SMEM,
        ],
        out_specs=[pair_spec(block, width)] * inner + [whole(half)] * 2,
        scratch_shapes=[pltpu.VMEM((rows, PADDED, width), F32)],
        compiler_params=params(),
        cost_estimate=cost(1000, 1000),
    )(biomass, weights, odd)


def cell_update(mine, rest, odd, enz, sub, mono, enz_loss, vmax, kmich, khalf, enz_target):
    n_enz, rows, width = enz.shape
    n_sub, n_mono = sub.shape[0], mono.shape[0]

    def kernel(*refs):
        mine, rest, enz, sub, mono, side, loss, vmax, kmich, khalf, target = refs[:11]
        pool, left, mono_two, out, sums, speed, rate, share = refs[11:]
        half = mine.shape[0]

        @pl.when(side[0] == 0)
        def _():
            sums[:half] = mine[...]
            sums[half:] = rest[...]

        @pl.when(side[0] != 0)
        def _():
            sums[:half] = rest[...]
            sums[half:] = mine[...]

        rate[...] = jnp.zeros_like(rate)
        for e in range(n_enz):
            now = enz[e] * (1.0 - loss[e]) + sums[e]
            pool[e] = now
            speed[e] = vmax[e] * now / (kmich[e] + sub[target[e]])
        for e in range(n_enz):
            rate[target[e]] += speed[e]

        def finish(m, mono_one):
            demand = sums[n_enz + m]
            part = mono_one / (khalf[m] + demand + mono_one)
            mono_two[m] = mono_one - demand * part
            share[m] = part

        for s in range(n_sub):
            kept = sub[s] * jnp.exp(-rate[s])
            left[s] = kept
            finish(s, mono[s] + (sub[s] - kept))
        for m in range(n_sub, n_mono):
            finish(m, mono[m])
        share[n_mono] = jnp.ones((rows, width), F32)
        for m in range(n_mono + 1, SLOTS):
            share[m] = jnp.zeros((rows, width), F32)
        out[...] = jnp.swapaxes(share[...], 0, 1)

    vmem = pl.BlockSpec(memory_space=pltpu.VMEM)
    return pl.pallas_call(
        kernel,
        name="cell_update",
        out_shape=[
            jax.ShapeDtypeStruct(enz.shape, F32),
            jax.ShapeDtypeStruct(sub.shape, F32),
            jax.ShapeDtypeStruct(mono.shape, F32),
            jax.ShapeDtypeStruct((rows, SLOTS, width), F32),
        ],
        in_specs=[vmem] * 5 + [SMEM] * 6,
        out_specs=[vmem] * 4,
        scratch_shapes=[
            pltpu.VMEM((CHAN, rows, width), F32),
            pltpu.VMEM(enz.shape, F32),
            pltpu.VMEM(sub.shape, F32),
            pltpu.VMEM((SLOTS, rows, width), F32),
        ],
        compiler_params=params(),
        cost_estimate=cost(1000, 1000),
    )(mine, rest, enz, sub, mono, odd, enz_loss, vmax, kmich, khalf, enz_target)


def store_pieces(pieces, index, value):
    count, width = value.shape
    columns = slice(width * index, width * (index + 1))
    high, low = split(value, 2)
    pieces[:count, columns] = high
    pieces[count:, columns] = low


def stencil(pieces, circulant, first, count, offset):
    width = circulant.shape[1]
    both = matmul(
        pieces[:, width * first : width * (first + count)],
        circulant[width * offset : width * (offset + count), :],
    )
    half = both.shape[0] // 2
    return both[:half] + both[half:]


def window(target, rows):
    first = max(target - 2, 0)
    return first, min(target + 2, rows - 1) - first + 1, first - target + 2


def spread(value, fraction, change):
    return value + jnp.concatenate([fraction, fraction], 1) * change


def whole(shape):
    return pl.BlockSpec(shape, lambda i: (0,) * len(shape))


def pair_spec(block, width, at=0):
    return pl.BlockSpec((2, block, width), lambda i: (at, i, 0))


def taxa_spec(block, width):
    return pl.BlockSpec((block, width), lambda i: (i, 0))


def day_one_inside(row_pairs, share, gain, fraction, circulant, weights, block):
    _, count, width = row_pairs[0].shape
    rows = 2 * len(row_pairs)
    inner = rows - 4

    def kernel(*refs):
        pairs = refs[: len(row_pairs)]
        own, gain_w, frac, circ, weight, out, to_next, to_previous, total, pieces = refs[len(row_pairs) :]

        @pl.when(pl.program_id(0) == 0)
        def _():
            total[...] = jnp.zeros_like(total)

        for row in range(rows):
            value = pairs[row // 2][row % 2] * matmul(gain_w[...], share_operand(own[row]))
            out[row] = value
            store_pieces(pieces, row, value)
        for row in range(rows):
            value = spread(out[row], frac[...], stencil(pieces, circ, *window(row, rows)))
            out[row] = value
            if 2 <= row < rows - 2:
                add_sums(total, row - 2, value, weight[...])
        for i, (source, number, offset) in enumerate(TERMS):
            source += rows - 4 if i < 2 else 0
            value = spread(0.0, frac[...], stencil(pieces, circ, source, number, offset))
            (to_next if i < 2 else to_previous)[i % 2] = value

    return pl.pallas_call(
        kernel,
        name="day_one_inside",
        grid=(count // block,),
        out_shape=[
            jax.ShapeDtypeStruct((rows, count, width), F32),
            *[jax.ShapeDtypeStruct((2, count, width), F32)] * 2,
            jax.ShapeDtypeStruct((inner, PADDED, width), F32),
        ],
        in_specs=[pair_spec(block, width)] * len(row_pairs)
        + [
            whole(share.shape),
            taxa_spec(block, gain.shape[1]),
            taxa_spec(block, HALF),
            whole(circulant.shape),
            pl.BlockSpec((2 * PADDED, block), lambda i: (0, i)),
        ],
        out_specs=[
            pl.BlockSpec((rows, block, width), lambda i: (0, i, 0)),
            pair_spec(block, width),
            pair_spec(block, width),
            whole((inner, PADDED, width)),
        ],
        scratch_shapes=[pltpu.VMEM((2 * block, rows * width), BF16)],
        compiler_params=params(),
        cost_estimate=cost(1000, 1000),
    )(*row_pairs, share, gain, fraction, circulant, weights)


TERMS = ((0, 2, 0), (1, 1, 0), (2, 1, 4), (2, 2, 3))


def day_one_rim(low, high, inside, sums, share_low, share_high, gain, fraction, circulant, weights, odd, block):
    _, count, width = low.shape
    rows = inside.shape[0]

    def kernel(
        low, high, first, last, part, before, after, gain_w, frac, circ, weight, side, out, mine, other, far, total
    ):
        @pl.when(pl.program_id(0) == 0)
        def _():
            total[2 : rows - 2] = part[...]
            for row in (0, 1, rows - 2, rows - 1):
                total[row] = jnp.zeros((PADDED, width), F32)

        for i in range(4):
            x = low[i] if i < 2 else high[i - 2]
            s = before[i] if i < 2 else after[i - 2]
            store_pieces(far, i, x * matmul(gain_w[...], share_operand(s)))
        for i in range(4):
            x = first[i] if i < 2 else last[i - 2]
            value = spread(x, frac[...], stencil(far, circ, *TERMS[i]))
            out[i] = value
            add_sums(total, i if i < 2 else rows - 4 + i, value, weight[...])

        @pl.when(pl.program_id(0) == pl.num_programs(0) - 1)
        def _():
            finish_sums(total, side, mine, other)

    half = (CHAN // 2, rows, width)
    return pl.pallas_call(
        kernel,
        name="day_one_rim",
        grid=(count // block,),
        out_shape=[jax.ShapeDtypeStruct((4, count, width), F32)] + [jax.ShapeDtypeStruct(half, F32)] * 2,
        in_specs=[
            pair_spec(block, width),
            pair_spec(block, width),
            pair_spec(block, width),
            pair_spec(block, width, rows // 2 - 1),
            whole(sums.shape),
            whole(share_low.shape),
            whole(share_high.shape),
            taxa_spec(block, gain.shape[1]),
            taxa_spec(block, HALF),
            whole(circulant.shape),
            pl.BlockSpec((2 * PADDED, block), lambda i: (0, i)),
            SMEM,
        ],
        out_specs=[pl.BlockSpec((4, block, width), lambda i: (0, i, 0))] + [whole(half)] * 2,
        scratch_shapes=[
            pltpu.VMEM((2 * block, 4 * width), BF16),
            pltpu.VMEM((rows, PADDED, width), F32),
        ],
        compiler_params=params(),
        cost_estimate=cost(1000, 1000),
    )(low, high, inside, inside, sums, share_low, share_high, gain, fraction, circulant, weights, odd)


def day_one_beyond(row_pairs, low, high, share, share_low, share_high, gain, fraction, circulant, block):
    _, count, width = low.shape
    rows = 2 * len(row_pairs)

    def kernel(low, high, first, last, own, before, after, gain_w, frac, circ, out, pieces):
        for side in range(2):
            for i in range(4):
                if side == 0:
                    x = low[i] if i < 2 else first[i - 2]
                    s = before[i] if i < 2 else own[i - 2]
                else:
                    x = last[i] if i < 2 else high[i - 2]
                    s = own[rows - 2 + i] if i < 2 else after[i - 2]
                value = x * matmul(gain_w[...], share_operand(s))
                store_pieces(pieces, i, value)
                if (i < 2) == (side == 0):
                    out[i] = value
            for i in (0, 1) if side == 0 else (2, 3):
                out[i] = spread(out[i], frac[...], stencil(pieces, circ, *window(i, 4)))

    return pl.pallas_call(
        kernel,
        name="day_one_beyond",
        grid=(count // block,),
        out_shape=jax.ShapeDtypeStruct((4, count, width), F32),
        in_specs=[pair_spec(block, width)] * 4
        + [
            whole(share.shape),
            whole(share_low.shape),
            whole(share_high.shape),
            taxa_spec(block, gain.shape[1]),
            taxa_spec(block, HALF),
            whole(circulant.shape),
        ],
        out_specs=pl.BlockSpec((4, block, width), lambda i: (0, i, 0)),
        scratch_shapes=[pltpu.VMEM((2 * block, 4 * width), BF16)],
        compiler_params=params(),
        cost_estimate=cost(1000, 1000),
    )(low, high, row_pairs[0], row_pairs[-1], share, share_low, share_high, gain, fraction, circulant)


def day_two(inside, rim, share, gain, fraction, circulant, block):
    rows, count, width = inside.shape
    steps = count // block
    middle = rows // 2 - 2

    def kernel(*refs):
        inner = refs[:middle]
        outer, own, gain_w, frac, circ, out, edge, pieces, result, sem = refs[middle:]
        step = pl.program_id(0)
        slot = lax.rem(step, 2)

        def copies(at, where):
            found = []
            taxa = pl.ds(pl.multiple_of(at * block, block), block)
            for row in range(rows):
                if 2 <= row < rows - 2:
                    target = out.at[taxa, row, :]
                else:
                    target = edge.at[row if row < 2 else row - rows + 4, taxa, :]
                found.append(pltpu.make_async_copy(result.at[where, row], target, sem.at[where, row]))
            return found

        @pl.when(step >= 2)
        def _():
            for copy in copies(step - 2, slot):
                copy.wait()

        for row in range(rows):
            if 2 <= row < rows - 2:
                x = inner[row // 2 - 1][row % 2]
            else:
                x = outer[row if row < 2 else row - rows + 4]
            value = x * matmul(gain_w[...], share_operand(own[row]))
            result[slot, row] = value
            store_pieces(pieces, row, value)
        for row in range(rows):
            result[slot, row] = spread(result[slot, row], frac[...], stencil(pieces, circ, *window(row, rows)))
        for copy in copies(step, slot):
            copy.start()

        @pl.when(step == steps - 1)
        def _():
            if steps > 1:
                for copy in copies(step - 1, 1 - slot):
                    copy.wait()
            for copy in copies(step, slot):
                copy.wait()

    return pl.pallas_call(
        kernel,
        name="day_two",
        grid=(steps,),
        out_shape=[
            jax.ShapeDtypeStruct((count, rows, width), F32),
            jax.ShapeDtypeStruct((4, count, width), F32),
        ],
        in_specs=[
            *[pair_spec(block, width, 1 + i) for i in range(middle)],
            pl.BlockSpec((4, block, width), lambda i: (0, i, 0)),
            whole(share.shape),
            taxa_spec(block, gain.shape[1]),
            taxa_spec(block, HALF),
            whole(circulant.shape),
        ],
        out_specs=[ANY, ANY],
        scratch_shapes=[
            pltpu.VMEM((2 * block, rows * width), BF16),
            pltpu.VMEM((2, rows, block, width), F32),
            pltpu.SemaphoreType.DMA((2, rows)),
        ],
        compiler_params=params(),
        cost_estimate=cost(1000, 1000),
    )(*[inside] * middle, rim, share, gain, fraction, circulant)


def edges(early_low, late_low, from_high, beyond, edge, biomass_out, share_low, share_high, gain, fraction, circulant, block):
    _, count, width = from_high.shape
    rows = biomass_out.shape[1]
    steps = count // block

    def kernel(
        early, late, high, near_low, near_high, own, before, after, gain_w, frac, circ, unused, out, near, result, sem
    ):
        step = pl.program_id(0)
        slot = lax.rem(step, 2)

        def copies(at, where):
            taxa = pl.ds(pl.multiple_of(at * block, block), block)
            return [
                pltpu.make_async_copy(
                    result.at[where, i],
                    out.at[taxa, i if i < 2 else rows - 4 + i, :],
                    sem.at[where, i],
                )
                for i in range(4)
            ]

        @pl.when(step >= 2)
        def _():
            for copy in copies(step - 2, slot):
                copy.wait()

        started = copies(step, slot)
        for side in ((0, 1), (2, 3)):
            for i in side:
                if i < 2:
                    value = near_low[i] + jnp.where(step == 0, early[i], late[i])
                else:
                    value = near_high[i - 2] + high[i - 2]
                s = before[i] if i < 2 else after[i - 2]
                store_pieces(near, i, value * matmul(gain_w[...], share_operand(s)))
            for i in side:
                result[slot, i] = spread(own[i], frac[...], stencil(near, circ, *TERMS[i]))
            for i in side:
                started[i].start()

        @pl.when(step == steps - 1)
        def _():
            if steps > 1:
                for copy in copies(step - 1, 1 - slot):
                    copy.wait()
            for copy in copies(step, slot):
                copy.wait()

    return pl.pallas_call(
        kernel,
        name="edges",
        grid=(steps,),
        out_shape=jax.ShapeDtypeStruct(biomass_out.shape, F32),
        in_specs=[
            whole(early_low.shape),
            whole(late_low.shape),
            pair_spec(block, width),
            pl.BlockSpec((2, block, width), lambda i: (0, i, 0)),
            pl.BlockSpec((2, block, width), lambda i: (1, i, 0)),
            pl.BlockSpec((4, block, width), lambda i: (0, i, 0)),
            whole(share_low.shape),
            whole(share_high.shape),
            pl.BlockSpec((block, gain.shape[1]), lambda i: (i, 0)),
            pl.BlockSpec((block, HALF), lambda i: (i, 0)),
            whole(circulant.shape),
            ANY,
        ],
        out_specs=ANY,
        scratch_shapes=[
            pltpu.VMEM((2 * block, 4 * width), BF16),
            pltpu.VMEM((2, 4, block, width), F32),
            pltpu.SemaphoreType.DMA((2, 4)),
        ],
        input_output_aliases={11: 0},
        compiler_params=params(),
        cost_estimate=cost(1000, 1000),
    )(
        early_low,
        late_low,
        from_high,
        beyond,
        beyond,
        edge,
        share_low,
        share_high,
        gain,
        fraction,
        circulant,
        biomass_out,
    )


def over_taxa(mine, other):
    count = lax.axis_size("taxa")

    def exchange(x, step):
        return lax.ppermute(x, "taxa", [(i, i ^ step) for i in range(count)])

    mine = mine + exchange(other, 1)
    step = 2
    while step < count:
        mine = mine + exchange(mine, step)
        step *= 2
    return mine, exchange(mine, 1)


def as_branch(offsets, run, *operands):
    def unused(*operands):
        return jax.tree.map(lambda x: jnp.zeros(x.shape, x.dtype), jax.eval_shape(run, *operands))

    return lax.cond(offsets[0, 0] < 3, run, unused, *operands)


def body(
    biomass,
    enzymes,
    substrates,
    monomers,
    enz_traits,
    mono_traits,
    enz_target,
    prod_rate,
    uptake_rate,
    mortality,
    disperse,
    enz_loss,
    vmax,
    kmich,
    khalf,
    offsets,
):
    ring = lax.axis_size("space")
    forward = [(i, (i + 1) % ring) for i in range(ring)]
    backward = [(target, source) for source, target in forward]

    def down(x):
        return lax.ppermute(x, "space", forward)

    def up(x):
        return lax.ppermute(x, "space", backward)

    count, rows, width = biomass.shape
    block = min(count, 256)

    first, last = take_first(biomass, (0, 1, rows - 2, rows - 1), 4)
    inner_low, inner_high = down(last), up(first)
    odd = lax.rem(lax.axis_index("taxa"), 2).reshape(1).astype(jnp.int32)
    traits = (enz_traits.T, mono_traits.T, prod_rate.reshape(1, count), uptake_rate.reshape(1, count))
    cells = (enz_loss, vmax, kmich, khalf, enz_target)

    def sums_and_cells(biomass, enzymes, substrates, monomers):
        weights = sum_weights(*traits)
        *middle, mine, other = first_sums(biomass, weights, odd, block)
        sums = over_taxa(mine, other)
        return *middle, weights, *cell_update(*sums, odd, enzymes, substrates, monomers, *cells)

    *middle, weights, enzymes, substrates, monomers, share_one = as_branch(
        offsets, sums_and_cells, biomass, enzymes, substrates, monomers
    )
    row_pairs = [first, *middle, last]
    spreading = spread_operands(
        *traits, mortality.reshape(1, count), disperse.reshape(1, count), offsets, width
    )
    share_low, share_high = down(share_one[rows - 2 :]), up(share_one[:2])
    inside, to_next, to_previous, inside_sums = day_one_inside(row_pairs, share_one, *spreading, weights, block)

    early = count // 2
    inner_low, inner_high, share_low, share_high, inside, next_early, to_previous = lax.optimization_barrier(
        (inner_low, inner_high, share_low, share_high, inside, to_next[:, :early], to_previous)
    )
    from_low, from_high = down(next_early), up(to_previous)

    def rest_of_day_one(low, high, share_low, share_high, enzymes, substrates, monomers):
        rim, *sums = day_one_rim(
            low, high, inside, inside_sums, share_low, share_high, *spreading, weights, odd, block
        )
        sums = over_taxa(*sums)
        return rim, *cell_update(*sums, odd, enzymes, substrates, monomers, *cells)

    rim, enzymes, substrates, monomers, share_two = as_branch(
        offsets,
        rest_of_day_one,
        inner_low,
        inner_high,
        share_low,
        share_high,
        enzymes,
        substrates,
        monomers,
    )
    near_low, near_high = down(share_two[rows - 2 :]), up(share_two[:2])
    inner_low, inner_high, share_two = lax.optimization_barrier((inner_low, inner_high, share_two))
    beyond = day_one_beyond(
        row_pairs, inner_low, inner_high, share_one, share_low, share_high, *spreading, block
    )
    beyond, next_late = lax.optimization_barrier((beyond, to_next[:, early:]))
    late_low = down(next_late)
    biomass_out, edge = day_two(inside, rim, share_two, *spreading, block)
    biomass_out = edges(
        from_low, late_low, from_high, beyond, edge, biomass_out, near_low, near_high, *spreading, early
    )
    return (biomass_out, enzymes, substrates, monomers)


def solution(mesh):
    placed = (
        P("taxa", "space", None),
        P(None, "space", None),
        P(None, "space", None),
        P(None, "space", None),
        P("taxa", None),
        P("taxa", None),
        P(),
        P("taxa"),
        P("taxa"),
        P("taxa"),
        P("taxa"),
        P(),
        P(),
        P(),
        P(),
        P(),
    )
    return jax.shard_map(
        body,
        mesh=mesh,
        in_specs=placed,
        out_specs=(
            P("taxa", "space", None),
            P(None, "space", None),
            P(None, "space", None),
            P(None, "space", None),
        ),
        check_vma=False,
    )
```

```python
import jax
import jax.numpy as jnp
from jax import lax
from jax.experimental import pallas as pl
from jax.experimental.pallas import tpu as pltpu
from jax.sharding import PartitionSpec as P

KOFF = 8
YIELD = 0.6
HALF = 128
SLOTS = 16
CHAN = 56
PADDED = 64
F32 = jnp.float32
BF16 = jnp.bfloat16
ANY = pl.BlockSpec(memory_space=pl.ANY)
SMEM = pl.BlockSpec(memory_space=pltpu.SMEM)
VMEM_BYTES = 40 << 20


def params():
    return pltpu.CompilerParams(vmem_limit_bytes=VMEM_BYTES)


def cost(flops, moved):
    return pl.CostEstimate(flops=flops, bytes_accessed=moved, transcendentals=0)


def split(x, count):
    out = []
    for _ in range(count):
        part = x.astype(BF16)
        out.append(part)
        x = x - part.astype(F32)
    return out


def share_operand(share):
    high, mid, low = split(share, 3)
    return jnp.concatenate([high, mid, low, high, mid, high], 0)


def matmul(a, b):
    return jnp.dot(a, b, preferred_element_type=F32)


def take_first(biomass, rows, pieces):
    count, height, width = biomass.shape
    pairs = len(rows) // 2
    step = count // pieces

    def kernel(source, *refs):
        outs, held, arrived, left = refs[:pairs], refs[pairs], refs[pairs + 1], refs[pairs + 2]
        loads, stores = [], []
        for p in range(pieces):
            taxa = pl.ds(p * step, step)
            loads.append(pltpu.make_async_copy(source.at[taxa], held.at[taxa], arrived.at[p]))
            loads[-1].start()
        for p in range(pieces):
            taxa = pl.ds(p * step, step)
            loads[p].wait()
            for i, row in enumerate(rows):
                stores.append(
                    pltpu.make_async_copy(held.at[taxa, row, :], outs[i // 2].at[i % 2, taxa], left.at[p, i])
                )
                stores[-1].start()
        for copy in stores:
            copy.wait()

    return pl.pallas_call(
        kernel,
        name="take_first",
        out_shape=[jax.ShapeDtypeStruct((2, count, width), F32)] * pairs,
        in_specs=[ANY],
        out_specs=[ANY] * pairs,
        scratch_shapes=[
            pltpu.VMEM((count, height, width), F32),
            pltpu.SemaphoreType.DMA((pieces,)),
            pltpu.SemaphoreType.DMA((pieces, len(rows))),
        ],
        compiler_params=pltpu.CompilerParams(vmem_limit_bytes=60 << 20),
        cost_estimate=cost(1000, 1000),
    )(biomass)


def add_sums(total, row, x, weights):
    high, low = split(x, 2)
    first = matmul(weights, high)
    second = matmul(weights[:PADDED], low)
    total[row] += first[:PADDED] + first[PADDED:] + second


def finish_sums(total, odd, mine, other):
    low = jnp.swapaxes(total[:, : CHAN // 2, :], 0, 1)
    high = jnp.swapaxes(total[:, CHAN // 2 : CHAN, :], 0, 1)

    @pl.when(odd[0] == 0)
    def _():
        mine[...] = low
        other[...] = high

    @pl.when(odd[0] != 0)
    def _():
        mine[...] = high
        other[...] = low


def sum_weights(enz_traits, mono_traits, prod_rate, uptake_rate):
    n_enz, count = enz_traits.shape
    used = n_enz + mono_traits.shape[0]

    def kernel(enz, mono, prod, uptake, out, held):
        held[:n_enz] = enz[...].astype(F32) * prod[...]
        held[n_enz:used] = mono[...].astype(F32) * uptake[...]
        held[used:] = jnp.zeros((PADDED - used, count), F32)
        high, low = split(held[...], 2)
        out[:PADDED] = high
        out[PADDED:] = low

    return pl.pallas_call(
        kernel,
        name="sum_weights",
        out_shape=jax.ShapeDtypeStruct((2 * PADDED, count), BF16),
        scratch_shapes=[pltpu.VMEM((PADDED, count), F32)],
        compiler_params=params(),
        cost_estimate=cost(1000, 1000),
    )(enz_traits, mono_traits, prod_rate, uptake_rate)


def spread_operands(enz_traits, mono_traits, prod_rate, uptake_rate, mortality, disperse, offsets, width):
    count = enz_traits.shape[1]
    n_mono = mono_traits.shape[0]

    def kernel(enz, mono, prod, uptake, mort, disp, offs, gain, fraction, circulant, held, stacked):
        held[...] = jnp.zeros_like(held)
        held[:n_mono] = (YIELD * uptake[...]) * mono[...].astype(F32)
        made = jnp.sum(enz[...].astype(F32), axis=0, keepdims=True)
        held[n_mono : n_mono + 1] = 1.0 - mort[...] - prod[...] * made
        high, mid, low = (part.astype(F32) for part in split(held[...], 3))
        stacked[...] = jnp.zeros_like(stacked)
        for i, part in enumerate((high, high, high, mid, mid, low)):
            stacked[SLOTS * i : SLOTS * (i + 1)] = part
        gain[...] = stacked[...].T[:, : 6 * SLOTS].astype(BF16)
        fraction[...] = jnp.broadcast_to(disp[...] * (1.0 / KOFF), (HALF, count)).T
        source = lax.broadcasted_iota(jnp.int32, (width, width), 0)
        target = lax.broadcasted_iota(jnp.int32, (width, width), 1)
        apart = (target - source + width + 2) & (width - 1)
        for i in range(5):
            total = jnp.zeros((width, width), F32)
            for j in range(5):
                number = jnp.int32(-KOFF if i == 2 and j == 2 else 0)
                for k in range(KOFF):
                    hit = (offs[k, 0] == 2 - i) & (offs[k, 1] == j - 2)
                    number = number + hit.astype(jnp.int32)
                total = jnp.where(apart == j, number.astype(F32), total)
            circulant[width * i : width * (i + 1)] = total.astype(BF16)

    vmem = pl.BlockSpec(memory_space=pltpu.VMEM)
    return pl.pallas_call(
        kernel,
        name="spread_operands",
        out_shape=[
            jax.ShapeDtypeStruct((count, 6 * SLOTS), BF16),
            jax.ShapeDtypeStruct((count, HALF), F32),
            jax.ShapeDtypeStruct((5 * width, width), BF16),
        ],
        in_specs=[vmem] * 6 + [SMEM],
        out_specs=[vmem] * 3,
        scratch_shapes=[pltpu.VMEM((SLOTS, count), F32), pltpu.VMEM((HALF, count), F32)],
        compiler_params=params(),
        cost_estimate=cost(1000, 1000),
    )(enz_traits, mono_traits, prod_rate, uptake_rate, mortality, disperse, offsets)


def first_sums(biomass, weights, odd, block):
    count, rows, width = biomass.shape
    inner = rows // 2 - 2

    def kernel(source, weight, side, *refs):
        pairs, (mine, other, total) = refs[:inner], refs[inner:]

        @pl.when(pl.program_id(0) == 0)
        def _():
            total[...] = jnp.zeros_like(total)

        x = jnp.swapaxes(source[...], 0, 1)
        for row in range(rows):
            if 2 <= row < rows - 2:
                pairs[row // 2 - 1][row % 2] = x[row]
            add_sums(total, row, x[row], weight[...])

        @pl.when(pl.program_id(0) == pl.num_programs(0) - 1)
        def _():
            finish_sums(total, side, mine, other)

    half = (CHAN // 2, rows, width)
    return pl.pallas_call(
        kernel,
        name="first_sums",
        grid=(count // block,),
        out_shape=[jax.ShapeDtypeStruct((2, count, width), F32)] * inner + [jax.ShapeDtypeStruct(half, F32)] * 2,
        in_specs=[
            pl.BlockSpec((block, rows, width), lambda i: (i, 0, 0)),
            pl.BlockSpec((2 * PADDED, block), lambda i: (0, i)),
            SMEM,
        ],
        out_specs=[pair_spec(block, width)] * inner + [whole(half)] * 2,
        scratch_shapes=[pltpu.VMEM((rows, PADDED, width), F32)],
        compiler_params=params(),
        cost_estimate=cost(1000, 1000),
    )(biomass, weights, odd)


def cell_update(mine, rest, odd, enz, sub, mono, enz_loss, vmax, kmich, khalf, enz_target):
    n_enz, rows, width = enz.shape
    n_sub, n_mono = sub.shape[0], mono.shape[0]

    def kernel(*refs):
        mine, rest, enz, sub, mono, side, loss, vmax, kmich, khalf, target = refs[:11]
        pool, left, mono_two, out, sums, speed, rate, share = refs[11:]
        half = mine.shape[0]

        @pl.when(side[0] == 0)
        def _():
            sums[:half] = mine[...]
            sums[half:] = rest[...]

        @pl.when(side[0] != 0)
        def _():
            sums[:half] = rest[...]
            sums[half:] = mine[...]

        rate[...] = jnp.zeros_like(rate)
        for e in range(n_enz):
            now = enz[e] * (1.0 - loss[e]) + sums[e]
            pool[e] = now
            speed[e] = vmax[e] * now / (kmich[e] + sub[target[e]])
        for e in range(n_enz):
            rate[target[e]] += speed[e]

        def finish(m, mono_one):
            demand = sums[n_enz + m]
            part = mono_one / (khalf[m] + demand + mono_one)
            mono_two[m] = mono_one - demand * part
            share[m] = part

        for s in range(n_sub):
            kept = sub[s] * jnp.exp(-rate[s])
            left[s] = kept
            finish(s, mono[s] + (sub[s] - kept))
        for m in range(n_sub, n_mono):
            finish(m, mono[m])
        share[n_mono] = jnp.ones((rows, width), F32)
        for m in range(n_mono + 1, SLOTS):
            share[m] = jnp.zeros((rows, width), F32)
        out[...] = jnp.swapaxes(share[...], 0, 1)

    vmem = pl.BlockSpec(memory_space=pltpu.VMEM)
    return pl.pallas_call(
        kernel,
        name="cell_update",
        out_shape=[
            jax.ShapeDtypeStruct(enz.shape, F32),
            jax.ShapeDtypeStruct(sub.shape, F32),
            jax.ShapeDtypeStruct(mono.shape, F32),
            jax.ShapeDtypeStruct((rows, SLOTS, width), F32),
        ],
        in_specs=[vmem] * 5 + [SMEM] * 6,
        out_specs=[vmem] * 4,
        scratch_shapes=[
            pltpu.VMEM((CHAN, rows, width), F32),
            pltpu.VMEM(enz.shape, F32),
            pltpu.VMEM(sub.shape, F32),
            pltpu.VMEM((SLOTS, rows, width), F32),
        ],
        compiler_params=params(),
        cost_estimate=cost(1000, 1000),
    )(mine, rest, enz, sub, mono, odd, enz_loss, vmax, kmich, khalf, enz_target)


def store_pieces(pieces, index, value):
    count, width = value.shape
    columns = slice(width * index, width * (index + 1))
    high, low = split(value, 2)
    pieces[:count, columns] = high
    pieces[count:, columns] = low


def stencil(pieces, circulant, first, count, offset):
    width = circulant.shape[1]
    both = matmul(
        pieces[:, width * first : width * (first + count)],
        circulant[width * offset : width * (offset + count), :],
    )
    half = both.shape[0] // 2
    return both[:half] + both[half:]


def window(target, rows):
    first = max(target - 2, 0)
    return first, min(target + 2, rows - 1) - first + 1, first - target + 2


def spread(value, fraction, change):
    return value + jnp.concatenate([fraction, fraction], 1) * change


def whole(shape):
    return pl.BlockSpec(shape, lambda i: (0,) * len(shape))


def pair_spec(block, width, at=0):
    return pl.BlockSpec((2, block, width), lambda i: (at, i, 0))


def taxa_spec(block, width):
    return pl.BlockSpec((block, width), lambda i: (i, 0))


def day_one_inside(row_pairs, share, gain, fraction, circulant, weights, block):
    _, count, width = row_pairs[0].shape
    rows = 2 * len(row_pairs)
    inner = rows - 4

    def kernel(*refs):
        pairs = refs[: len(row_pairs)]
        own, gain_w, frac, circ, weight, out, to_next, to_previous, total, pieces = refs[len(row_pairs) :]

        @pl.when(pl.program_id(0) == 0)
        def _():
            total[...] = jnp.zeros_like(total)

        for row in range(rows):
            value = pairs[row // 2][row % 2] * matmul(gain_w[...], share_operand(own[row]))
            out[row] = value
            store_pieces(pieces, row, value)
        for row in range(rows):
            value = spread(out[row], frac[...], stencil(pieces, circ, *window(row, rows)))
            out[row] = value
            if 2 <= row < rows - 2:
                add_sums(total, row - 2, value, weight[...])
        for i, (source, number, offset) in enumerate(TERMS):
            source += rows - 4 if i < 2 else 0
            value = spread(0.0, frac[...], stencil(pieces, circ, source, number, offset))
            (to_next if i < 2 else to_previous)[i % 2] = value

    return pl.pallas_call(
        kernel,
        name="day_one_inside",
        grid=(count // block,),
        out_shape=[
            jax.ShapeDtypeStruct((rows, count, width), F32),
            *[jax.ShapeDtypeStruct((2, count, width), F32)] * 2,
            jax.ShapeDtypeStruct((inner, PADDED, width), F32),
        ],
        in_specs=[pair_spec(block, width)] * len(row_pairs)
        + [
            whole(share.shape),
            taxa_spec(block, gain.shape[1]),
            taxa_spec(block, HALF),
            whole(circulant.shape),
            pl.BlockSpec((2 * PADDED, block), lambda i: (0, i)),
        ],
        out_specs=[
            pl.BlockSpec((rows, block, width), lambda i: (0, i, 0)),
            pair_spec(block, width),
            pair_spec(block, width),
            whole((inner, PADDED, width)),
        ],
        scratch_shapes=[pltpu.VMEM((2 * block, rows * width), BF16)],
        compiler_params=params(),
        cost_estimate=cost(1000, 1000),
    )(*row_pairs, share, gain, fraction, circulant, weights)


TERMS = ((0, 2, 0), (1, 1, 0), (2, 1, 4), (2, 2, 3))


def day_one_rim(low, high, inside, sums, share_low, share_high, gain, fraction, circulant, weights, odd, block):
    _, count, width = low.shape
    rows = inside.shape[0]

    def kernel(
        low, high, first, last, part, before, after, gain_w, frac, circ, weight, side, out, mine, other, far, total
    ):
        @pl.when(pl.program_id(0) == 0)
        def _():
            total[2 : rows - 2] = part[...]
            for row in (0, 1, rows - 2, rows - 1):
                total[row] = jnp.zeros((PADDED, width), F32)

        for i in range(4):
            x = low[i] if i < 2 else high[i - 2]
            s = before[i] if i < 2 else after[i - 2]
            store_pieces(far, i, x * matmul(gain_w[...], share_operand(s)))
        for i in range(4):
            x = first[i] if i < 2 else last[i - 2]
            value = spread(x, frac[...], stencil(far, circ, *TERMS[i]))
            out[i] = value
            add_sums(total, i if i < 2 else rows - 4 + i, value, weight[...])

        @pl.when(pl.program_id(0) == pl.num_programs(0) - 1)
        def _():
            finish_sums(total, side, mine, other)

    half = (CHAN // 2, rows, width)
    return pl.pallas_call(
        kernel,
        name="day_one_rim",
        grid=(count // block,),
        out_shape=[jax.ShapeDtypeStruct((4, count, width), F32)] + [jax.ShapeDtypeStruct(half, F32)] * 2,
        in_specs=[
            pair_spec(block, width),
            pair_spec(block, width),
            pair_spec(block, width),
            pair_spec(block, width, rows // 2 - 1),
            whole(sums.shape),
            whole(share_low.shape),
            whole(share_high.shape),
            taxa_spec(block, gain.shape[1]),
            taxa_spec(block, HALF),
            whole(circulant.shape),
            pl.BlockSpec((2 * PADDED, block), lambda i: (0, i)),
            SMEM,
        ],
        out_specs=[pl.BlockSpec((4, block, width), lambda i: (0, i, 0))] + [whole(half)] * 2,
        scratch_shapes=[
            pltpu.VMEM((2 * block, 4 * width), BF16),
            pltpu.VMEM((rows, PADDED, width), F32),
        ],
        compiler_params=params(),
        cost_estimate=cost(1000, 1000),
    )(low, high, inside, inside, sums, share_low, share_high, gain, fraction, circulant, weights, odd)


def day_one_beyond(row_pairs, low, high, share, share_low, share_high, gain, fraction, circulant, block):
    _, count, width = low.shape
    rows = 2 * len(row_pairs)

    def kernel(low, high, first, last, own, before, after, gain_w, frac, circ, out, pieces):
        for side in range(2):
            for i in range(4):
                if side == 0:
                    x = low[i] if i < 2 else first[i - 2]
                    s = before[i] if i < 2 else own[i - 2]
                else:
                    x = last[i] if i < 2 else high[i - 2]
                    s = own[rows - 2 + i] if i < 2 else after[i - 2]
                value = x * matmul(gain_w[...], share_operand(s))
                store_pieces(pieces, i, value)
                if (i < 2) == (side == 0):
                    out[i] = value
            for i in (0, 1) if side == 0 else (2, 3):
                out[i] = spread(out[i], frac[...], stencil(pieces, circ, *window(i, 4)))

    return pl.pallas_call(
        kernel,
        name="day_one_beyond",
        grid=(count // block,),
        out_shape=jax.ShapeDtypeStruct((4, count, width), F32),
        in_specs=[pair_spec(block, width)] * 4
        + [
            whole(share.shape),
            whole(share_low.shape),
            whole(share_high.shape),
            taxa_spec(block, gain.shape[1]),
            taxa_spec(block, HALF),
            whole(circulant.shape),
        ],
        out_specs=pl.BlockSpec((4, block, width), lambda i: (0, i, 0)),
        scratch_shapes=[pltpu.VMEM((2 * block, 4 * width), BF16)],
        compiler_params=params(),
        cost_estimate=cost(1000, 1000),
    )(low, high, row_pairs[0], row_pairs[-1], share, share_low, share_high, gain, fraction, circulant)


def day_two(inside, rim, share, gain, fraction, circulant, block):
    rows, count, width = inside.shape
    steps = count // block
    middle = rows // 2 - 2

    def kernel(*refs):
        inner = refs[:middle]
        outer, own, gain_w, frac, circ, out, edge, pieces, result, sem = refs[middle:]
        step = pl.program_id(0)
        slot = lax.rem(step, 2)

        def copies(at, where):
            found = []
            taxa = pl.ds(pl.multiple_of(at * block, block), block)
            for row in range(rows):
                if 2 <= row < rows - 2:
                    target = out.at[taxa, row, :]
                else:
                    target = edge.at[row if row < 2 else row - rows + 4, taxa, :]
                found.append(pltpu.make_async_copy(result.at[where, row], target, sem.at[where, row]))
            return found

        @pl.when(step >= 2)
        def _():
            for copy in copies(step - 2, slot):
                copy.wait()

        for row in range(rows):
            if 2 <= row < rows - 2:
                x = inner[row // 2 - 1][row % 2]
            else:
                x = outer[row if row < 2 else row - rows + 4]
            value = x * matmul(gain_w[...], share_operand(own[row]))
            result[slot, row] = value
            store_pieces(pieces, row, value)
        for row in range(rows):
            result[slot, row] = spread(result[slot, row], frac[...], stencil(pieces, circ, *window(row, rows)))
        for copy in copies(step, slot):
            copy.start()

        @pl.when(step == steps - 1)
        def _():
            if steps > 1:
                for copy in copies(step - 1, 1 - slot):
                    copy.wait()
            for copy in copies(step, slot):
                copy.wait()

    return pl.pallas_call(
        kernel,
        name="day_two",
        grid=(steps,),
        out_shape=[
            jax.ShapeDtypeStruct((count, rows, width), F32),
            jax.ShapeDtypeStruct((4, count, width), F32),
        ],
        in_specs=[
            *[pair_spec(block, width, 1 + i) for i in range(middle)],
            pl.BlockSpec((4, block, width), lambda i: (0, i, 0)),
            whole(share.shape),
            taxa_spec(block, gain.shape[1]),
            taxa_spec(block, HALF),
            whole(circulant.shape),
        ],
        out_specs=[ANY, ANY],
        scratch_shapes=[
            pltpu.VMEM((2 * block, rows * width), BF16),
            pltpu.VMEM((2, rows, block, width), F32),
            pltpu.SemaphoreType.DMA((2, rows)),
        ],
        compiler_params=params(),
        cost_estimate=cost(1000, 1000),
    )(*[inside] * middle, rim, share, gain, fraction, circulant)


def edges(early_low, late_low, from_high, beyond, edge, biomass_out, share_low, share_high, gain, fraction, circulant, block):
    _, count, width = from_high.shape
    rows = biomass_out.shape[1]
    steps = count // block

    def kernel(
        early, late, high, near_low, near_high, own, before, after, gain_w, frac, circ, unused, out, near, result, sem
    ):
        step = pl.program_id(0)
        slot = lax.rem(step, 2)

        def copies(at, where):
            taxa = pl.ds(pl.multiple_of(at * block, block), block)
            return [
                pltpu.make_async_copy(
                    result.at[where, i],
                    out.at[taxa, i if i < 2 else rows - 4 + i, :],
                    sem.at[where, i],
                )
                for i in range(4)
            ]

        @pl.when(step >= 2)
        def _():
            for copy in copies(step - 2, slot):
                copy.wait()

        for i in range(4):
            if i < 2:
                value = near_low[i] + jnp.where(step == 0, early[i], late[i])
            else:
                value = near_high[i - 2] + high[i - 2]
            s = before[i] if i < 2 else after[i - 2]
            store_pieces(near, i, value * matmul(gain_w[...], share_operand(s)))
        for i in range(4):
            result[slot, i] = spread(own[i], frac[...], stencil(near, circ, *TERMS[i]))
        for copy in copies(step, slot):
            copy.start()

        @pl.when(step == steps - 1)
        def _():
            if steps > 1:
                for copy in copies(step - 1, 1 - slot):
                    copy.wait()
            for copy in copies(step, slot):
                copy.wait()

    return pl.pallas_call(
        kernel,
        name="edges",
        grid=(steps,),
        out_shape=jax.ShapeDtypeStruct(biomass_out.shape, F32),
        in_specs=[
            whole(early_low.shape),
            whole(late_low.shape),
            pair_spec(block, width),
            pl.BlockSpec((2, block, width), lambda i: (0, i, 0)),
            pl.BlockSpec((2, block, width), lambda i: (1, i, 0)),
            pl.BlockSpec((4, block, width), lambda i: (0, i, 0)),
            whole(share_low.shape),
            whole(share_high.shape),
            pl.BlockSpec((block, gain.shape[1]), lambda i: (i, 0)),
            pl.BlockSpec((block, HALF), lambda i: (i, 0)),
            whole(circulant.shape),
            ANY,
        ],
        out_specs=ANY,
        scratch_shapes=[
            pltpu.VMEM((2 * block, 4 * width), BF16),
            pltpu.VMEM((2, 4, block, width), F32),
            pltpu.SemaphoreType.DMA((2, 4)),
        ],
        input_output_aliases={11: 0},
        compiler_params=params(),
        cost_estimate=cost(1000, 1000),
    )(
        early_low,
        late_low,
        from_high,
        beyond,
        beyond,
        edge,
        share_low,
        share_high,
        gain,
        fraction,
        circulant,
        biomass_out,
    )


def over_taxa(mine, other):
    count = lax.axis_size("taxa")

    def exchange(x, step):
        return lax.ppermute(x, "taxa", [(i, i ^ step) for i in range(count)])

    mine = mine + exchange(other, 1)
    step = 2
    while step < count:
        mine = mine + exchange(mine, step)
        step *= 2
    return mine, exchange(mine, 1)


def as_branch(offsets, run, *operands):
    def unused(*operands):
        return jax.tree.map(lambda x: jnp.zeros(x.shape, x.dtype), jax.eval_shape(run, *operands))

    return lax.cond(offsets[0, 0] < 3, run, unused, *operands)


def body(
    biomass,
    enzymes,
    substrates,
    monomers,
    enz_traits,
    mono_traits,
    enz_target,
    prod_rate,
    uptake_rate,
    mortality,
    disperse,
    enz_loss,
    vmax,
    kmich,
    khalf,
    offsets,
):
    ring = lax.axis_size("space")
    forward = [(i, (i + 1) % ring) for i in range(ring)]
    backward = [(target, source) for source, target in forward]

    def down(x):
        return lax.ppermute(x, "space", forward)

    def up(x):
        return lax.ppermute(x, "space", backward)

    count, rows, width = biomass.shape
    block = min(count, 256)

    first, last = take_first(biomass, (0, 1, rows - 2, rows - 1), 2)
    inner_low, inner_high = down(last), up(first)
    odd = lax.rem(lax.axis_index("taxa"), 2).reshape(1).astype(jnp.int32)
    traits = (enz_traits.T, mono_traits.T, prod_rate.reshape(1, count), uptake_rate.reshape(1, count))
    cells = (enz_loss, vmax, kmich, khalf, enz_target)

    def sums_and_cells(biomass, enzymes, substrates, monomers):
        weights = sum_weights(*traits)
        *middle, mine, other = first_sums(biomass, weights, odd, block)
        sums = over_taxa(mine, other)
        return *middle, weights, *cell_update(*sums, odd, enzymes, substrates, monomers, *cells)

    *middle, weights, enzymes, substrates, monomers, share_one = as_branch(
        offsets, sums_and_cells, biomass, enzymes, substrates, monomers
    )
    row_pairs = [first, *middle, last]
    spreading = spread_operands(
        *traits, mortality.reshape(1, count), disperse.reshape(1, count), offsets, width
    )
    share_low, share_high = down(share_one[rows - 2 :]), up(share_one[:2])
    inside, to_next, to_previous, inside_sums = day_one_inside(row_pairs, share_one, *spreading, weights, block)

    early = count // 2
    inner_low, inner_high, share_low, share_high, inside, next_early, to_previous = lax.optimization_barrier(
        (inner_low, inner_high, share_low, share_high, inside, to_next[:, :early], to_previous)
    )
    from_low, from_high = down(next_early), up(to_previous)

    def rest_of_day_one(low, high, share_low, share_high, enzymes, substrates, monomers):
        rim, *sums = day_one_rim(
            low, high, inside, inside_sums, share_low, share_high, *spreading, weights, odd, block
        )
        sums = over_taxa(*sums)
        return rim, *cell_update(*sums, odd, enzymes, substrates, monomers, *cells)

    rim, enzymes, substrates, monomers, share_two = as_branch(
        offsets,
        rest_of_day_one,
        inner_low,
        inner_high,
        share_low,
        share_high,
        enzymes,
        substrates,
        monomers,
    )
    near_low, near_high = down(share_two[rows - 2 :]), up(share_two[:2])
    inner_low, inner_high, share_two = lax.optimization_barrier((inner_low, inner_high, share_two))
    beyond = day_one_beyond(
        row_pairs, inner_low, inner_high, share_one, share_low, share_high, *spreading, block
    )
    beyond, next_late = lax.optimization_barrier((beyond, to_next[:, early:]))
    late_low = down(next_late)
    biomass_out, edge = day_two(inside, rim, share_two, *spreading, block)
    biomass_out = edges(
        from_low, late_low, from_high, beyond, edge, biomass_out, near_low, near_high, *spreading, early
    )
    return (biomass_out, enzymes, substrates, monomers)


def solution(mesh):
    placed = (
        P("taxa", "space", None),
        P(None, "space", None),
        P(None, "space", None),
        P(None, "space", None),
        P("taxa", None),
        P("taxa", None),
        P(),
        P("taxa"),
        P("taxa"),
        P("taxa"),
        P("taxa"),
        P(),
        P(),
        P(),
        P(),
        P(),
    )
    return jax.shard_map(
        body,
        mesh=mesh,
        in_specs=placed,
        out_specs=(
            P("taxa", "space", None),
            P(None, "space", None),
            P(None, "space", None),
            P(None, "space", None),
        ),
        check_vma=False,
    )
```
